32 devices in a mesh: seq: 8 (over z, y), tensor: 4 (over x, core).
Axes of the slice: x: 2, y: 2, z: 4, core: 2. Of those that a mesh axis runs over, the one named last changes fastest.
Arguments:
- tokens_in: bfloat16 [8192, 2048], P(('seq', 'tensor')), may hold values from -6 to 6
- w_query: bfloat16 [2048, 256], P(None, 'tensor'), may hold values from -0.125 to 0.125
- w_key: bfloat16 [2048, 256], P(None, 'tensor'), may hold values from -0.125 to 0.125
- w_value: bfloat16 [2048, 2048], P(None, 'tensor'), may hold values from -0.125 to 0.125
- w_output: bfloat16 [2048, 2048], P('tensor'), may hold values from -0.125 to 0.125
- conv_taps: float32 [3, 2048], P(None, 'tensor'), may hold values from -3 to 3
- norm_gain: float32 [2048], P('tensor'), may hold values from 0.1 to 1.9
- grad_out: bfloat16 [8192, 2048], P(('seq', 'tensor')), may hold values from -6 to 6
Outputs:
- layer_out: bfloat16 [8192, 2048], P(('seq', 'tensor'))
- grad_in: bfloat16 [8192, 2048], P(('seq', 'tensor'))
- grad_wq: bfloat16 [2048, 256], P('seq', 'tensor')
- grad_wk: bfloat16 [2048, 256], P('seq', 'tensor')
- grad_wv: bfloat16 [2048, 2048], P('seq', 'tensor')
- grad_wo: bfloat16 [2048, 2048], P('tensor', 'seq')
- grad_taps: float32 [3, 2048], P(None, 'tensor')
- grad_gain: float32 [2048], P('tensor')
The draws below stay inside these ranges and needn't reach their ends.
All inputs are finite; a program needn't handle non-finite values.
Results may differ from the reference program's by a relative error of at most 0.018.
Values may be sent and summed in bfloat16 or wider, within the bound.
No kernel may reach another device: no remote copies, remote signals or barrier semaphores. Data moves between devices by JAX's collectives and lax.ppermute only.
A program may use at most 192 MiB of HBM per device.

```python
import math
import jax
import jax.numpy as jnp
import numpy as np
from jax import lax

D = 2048
HEADS = 16
VD = 128
FK = 16
TOK_DEV = 1024
TOKENS = 8192
N_SEQ = 8
N_TENSOR = 4


def with_spikes(values, rng, source, target, blocks, factor):
    owner, partner = [(jnp.arange(values.shape[position]) // (values.shape[position] // blocks)).reshape([-1 if axis == position else 1 for axis in range(values.ndim)]) for position in (source, target)]
    chosen = jax.random.permutation(rng, blocks)[partner]
    strong = (owner == chosen) | (owner == (partner + blocks // 2) % blocks)
    return jnp.where(strong, factor * values, values)


def block_levels(stream_key, shape, cuts, smallest, high):
    def one(dim, blocks):
        draws = jax.random.uniform(jax.random.fold_in(jax.random.fold_in(stream_key, 6), dim), (blocks,), jnp.float32, smallest / len(cuts), high / len(cuts))
        return jnp.repeat(jnp.exp(draws), shape[dim] // blocks).reshape((-1,) + (1,) * (len(shape) - dim - 1))

    gain = one(*cuts[0])
    for cut in cuts[1:]:
        gain = gain * one(*cut)
    return gain


def centred(own_key, dims, width, bound, pieces=(), held_as=jnp.bfloat16):
    entries = width * jax.random.normal(own_key, dims, jnp.float32)
    if pieces:
        entries = entries * block_levels(own_key, dims, pieces, -0.22, 0.18)
    return jnp.clip(entries, -bound, bound).astype(held_as)


def gaussian_with(rng, dims, spread, limit, shards, heavy, kind=jnp.bfloat16):
    values = spread * jax.random.normal(rng, dims, jnp.float32)
    if shards:
        values = values * block_levels(rng, dims, shards, -0.22, 0.18)
    return jnp.clip(with_spikes(values, jax.random.fold_in(rng, 3), *heavy), -limit, limit).astype(kind)


def setup_inputs(seed: int = 0) -> dict:
    streams_of = jax.random.split(jax.random.key(seed), 9)
    return {
        "tokens_in": gaussian_with(streams_of[0], (TOKENS, D), 1.0, 6.0, ((0, 32),), (0, 1, 32, 2.75)),
        "w_query": centred(streams_of[1], (D, HEADS * FK), D ** -0.5, 0.125, ((1, 4),)),
        "w_key": centred(streams_of[2], (D, HEADS * FK), D ** -0.5, 0.125, ((1, 4),)),
        "w_value": centred(streams_of[3], (D, D), D ** -0.5, 0.125, ((1, 4),)),
        "w_output": centred(streams_of[4], (D, D), D ** -0.5, 0.125, ((0, 4),)),
        "conv_taps": centred(streams_of[5], (3, D), 0.6, 3.0, ((1, 4),), jnp.float32),
        "norm_gain": jnp.clip(1.0 + 0.18 * jax.random.normal(streams_of[6], (D,), jnp.float32), 0.1, 1.9),
        "grad_out": gaussian_with(streams_of[7], (TOKENS, D), 1.0, 6.0, ((0, 32),), (0, 1, 32, 2.75)),
    }


precise = lax.Precision.HIGHEST

def pair_table(extent):
    selector = np.zeros((extent * extent, extent * (extent + 1) // 2), np.float32)
    column = 0
    for first_at in range(extent):
        for second_at in range(first_at, extent):
            factor = extent ** (-0.5)
            if first_at == second_at:
                factor = factor / math.sqrt(2.0)
            selector[first_at * extent + second_at, column] = factor
            column += 1
    return selector

def taylor_features(head_vecs):
    extent = head_vecs.shape[-1]
    selector = jnp.asarray(pair_table(extent))
    unit_col = jnp.ones(head_vecs.shape[:-1] + (1,), jnp.float32)
    linear = head_vecs * extent ** (-0.25)
    outer_prod = (head_vecs[..., :, None] * head_vecs[..., None, :]).reshape(head_vecs.shape[:-1] + (extent * extent,))
    squares = jnp.einsum('hlp,pq->hlq', outer_prod, selector, precision=precise)
    return jnp.concatenate([unit_col, linear, squares], axis=-1)

def split_heads(matrix, head_width):
    return matrix.reshape(matrix.shape[0], matrix.shape[1] // head_width, head_width).transpose(1, 0, 2)

def attend(queries, key_rows, mixed, carried_state, gain_vec):
    head_count = carried_state.shape[0]
    head_size = carried_state.shape[2]
    feat_width = queries.shape[1] // head_count
    length = queries.shape[0]
    query_heads = split_heads(queries, feat_width)
    key_heads = split_heads(key_rows, feat_width)
    value_heads = split_heads(mixed, head_size)
    scores = jnp.einsum('hlf,hmf->hlm', query_heads, key_heads, precision=precise) * feat_width ** (-0.5)
    positions = jnp.arange(length)
    causal = positions[:, None] >= positions[None, :]
    weights = jnp.where(causal[None], 1.0 + scores + 0.5 * scores * scores, 0.0).astype(jnp.bfloat16)
    weights = lax.optimization_barrier(weights).astype(jnp.float32)
    value_low = lax.optimization_barrier(value_heads.astype(jnp.bfloat16)).astype(jnp.float32)
    local_part = jnp.einsum('hlm,hme->hle', weights, value_low, precision=precise)
    carried_part = jnp.einsum('hlp,hpe->hle', taylor_features(query_heads), carried_state, precision=precise)
    summed = local_part + carried_part
    normed = summed * lax.rsqrt(lax.optimization_barrier(jnp.mean(summed * summed, axis=-1, keepdims=True)) + 1e-06)
    return normed.transpose(1, 0, 2).reshape(length, head_count * head_size) * gain_vec

def summarize(key_rows, mixed):
    head_count = mixed.shape[1] // VD
    key_heads = split_heads(key_rows, key_rows.shape[1] // head_count)
    value_heads = split_heads(mixed, VD)
    return jnp.einsum('hlp,hle->hpe', taylor_features(key_heads), value_heads, precision=precise)

def rounded(partial_term):
    return lax.optimization_barrier(partial_term.astype(jnp.bfloat16)).astype(jnp.float32)

def reference(tokens_in, w_query, w_key, w_value, w_output, conv_taps, norm_gain, grad_out):
    grad_scale = TOKENS ** (-0.5)
    queries = jnp.dot(tokens_in, w_query, preferred_element_type=jnp.float32).astype(jnp.bfloat16)
    key_rows = jnp.dot(tokens_in, w_key, preferred_element_type=jnp.float32).astype(jnp.bfloat16)
    values = jnp.dot(tokens_in, w_value, preferred_element_type=jnp.float32).astype(jnp.bfloat16)
    value_wide = values.astype(jnp.float32)
    padded_values = jnp.concatenate([jnp.zeros((2, D), jnp.float32), value_wide], axis=0)
    mixed = (conv_taps[0] * padded_values[2:] + conv_taps[1] * padded_values[1:-1] + conv_taps[2] * padded_values[:-2]).astype(jnp.bfloat16)

    def to_blocks(matrix):
        return matrix.reshape(N_SEQ, TOK_DEV, matrix.shape[1])
    query_blocks = to_blocks(queries.astype(jnp.float32))
    key_blocks = to_blocks(key_rows.astype(jnp.float32))
    mixed_blocks = to_blocks(mixed.astype(jnp.float32))
    local_states, state_pull = jax.vjp(jax.vmap(summarize), key_blocks, mixed_blocks)
    zero_state = jnp.zeros((1,) + local_states.shape[1:], jnp.float32)
    carried = jnp.concatenate([zero_state, jnp.cumsum(local_states, axis=0)[:-1]], axis=0)
    grad_attn = lax.dot_general(grad_out, w_output, (((1,), (1,)), ((), ())), preferred_element_type=jnp.float32).astype(jnp.bfloat16)
    grad_blocks = to_blocks(grad_attn.astype(jnp.float32))

    def block_grads(block_items):
        q_block, k_block, m_block, s_block, g_block = block_items
        result, pullback = jax.vjp(attend, q_block, k_block, m_block, s_block, norm_gain)
        return (result.astype(jnp.bfloat16),) + tuple(pullback(g_block))
    attn_blocks, grad_q1, grad_k1, grad_m1, grad_carried, gain_parts = lax.map(block_grads, (query_blocks, key_blocks, mixed_blocks, carried, grad_blocks))
    attn = attn_blocks.reshape(TOKENS, D)
    reverse_sums = jnp.cumsum(grad_carried[::-1], axis=0)[::-1]
    grad_state = jnp.concatenate([reverse_sums[1:], zero_state], axis=0)
    grad_k2, grad_m2 = state_pull(grad_state)
    grad_query = grad_q1.reshape(TOKENS, HEADS * FK).astype(jnp.bfloat16)
    grad_keys = (grad_k1 + grad_k2).reshape(TOKENS, HEADS * FK).astype(jnp.bfloat16)
    grad_mixed = (grad_m1 + grad_m2).reshape(TOKENS, D)
    padded_grad = jnp.concatenate([grad_mixed, jnp.zeros((2, D), jnp.float32)], axis=0)
    grad_values = (conv_taps[0] * padded_grad[:-2] + conv_taps[1] * padded_grad[1:-1] + conv_taps[2] * padded_grad[2:]).astype(jnp.bfloat16)
    grad_taps = grad_scale * jnp.stack([lax.optimization_barrier(jnp.sum(grad_mixed * padded_values[2:], axis=0)), lax.optimization_barrier(jnp.sum(grad_mixed * padded_values[1:-1], axis=0)), lax.optimization_barrier(jnp.sum(grad_mixed * padded_values[:-2], axis=0))])
    grad_gain = grad_scale * lax.optimization_barrier(jnp.sum(gain_parts, axis=0))
    value_group = D // N_TENSOR
    key_group = HEADS * FK // N_TENSOR
    contract_cols = (((1,), (1,)), ((), ()))

    def out_group(running, index):
        cols = lax.dynamic_slice_in_dim(attn, index * value_group, value_group, 1)
        rows_part = lax.dynamic_slice_in_dim(w_output, index * value_group, value_group, 0)
        return (running + rounded(jnp.dot(cols, rows_part, preferred_element_type=jnp.float32)), None)

    def in_group(running, index):
        total_part = lax.dot_general(lax.dynamic_slice_in_dim(grad_query, index * key_group, key_group, 1), lax.dynamic_slice_in_dim(w_query, index * key_group, key_group, 1), contract_cols, preferred_element_type=jnp.float32)
        total_part = total_part + lax.dot_general(lax.dynamic_slice_in_dim(grad_keys, index * key_group, key_group, 1), lax.dynamic_slice_in_dim(w_key, index * key_group, key_group, 1), contract_cols, preferred_element_type=jnp.float32)
        total_part = total_part + lax.dot_general(lax.dynamic_slice_in_dim(grad_values, index * value_group, value_group, 1), lax.dynamic_slice_in_dim(w_value, index * value_group, value_group, 1), contract_cols, preferred_element_type=jnp.float32)
        return (running + rounded(total_part), None)
    group_ids = jnp.arange(N_TENSOR, dtype=jnp.int32)
    layer_sum, _ = lax.scan(out_group, jnp.zeros((TOKENS, D), jnp.float32), group_ids)
    input_sum, _ = lax.scan(in_group, jnp.zeros((TOKENS, D), jnp.float32), group_ids)
    contract_rows = (((0,), (0,)), ((), ()))

    def weight_block(running, index):

        def block_rows(matrix):
            return lax.dynamic_slice_in_dim(matrix, index * TOK_DEV, TOK_DEV, 0)
        rows_x = block_rows(tokens_in)
        terms = (lax.dot_general(rows_x, block_rows(grad_query), contract_rows, preferred_element_type=jnp.float32), lax.dot_general(rows_x, block_rows(grad_keys), contract_rows, preferred_element_type=jnp.float32), lax.dot_general(rows_x, block_rows(grad_values), contract_rows, preferred_element_type=jnp.float32), lax.dot_general(block_rows(attn), block_rows(grad_out), contract_rows, preferred_element_type=jnp.float32))
        return (tuple((held + rounded(grad_scale * term_now) for held, term_now in zip(running, terms))), None)
    start_sums = (jnp.zeros((D, HEADS * FK), jnp.float32), jnp.zeros((D, HEADS * FK), jnp.float32), jnp.zeros((D, D), jnp.float32), jnp.zeros((D, D), jnp.float32))
    weight_totals, _ = lax.scan(weight_block, start_sums, jnp.arange(N_SEQ, dtype=jnp.int32))
    return (layer_sum.astype(jnp.bfloat16), input_sum.astype(jnp.bfloat16), weight_totals[0].astype(jnp.bfloat16), weight_totals[1].astype(jnp.bfloat16), weight_totals[2].astype(jnp.bfloat16), weight_totals[3].astype(jnp.bfloat16), grad_taps, grad_gain)
```

```python
import functools

import jax
import jax.numpy as jnp
import numpy as np
from jax import lax
from jax.experimental import pallas as pl
from jax.experimental.pallas import tpu as pltpu
from jax.sharding import PartitionSpec as P

VD = 128
FK = 16
FEATS = 153
STATE_ROWS = 160
LANES = 256
EPS = 1e-6

bf16 = jnp.bfloat16
f32 = jnp.float32
CONTRACT_COLS = (((1,), (1,)), ((), ()))
CONTRACT_ROWS = (((0,), (0,)), ((), ()))


def mm(a, b):
    return jnp.dot(a, b, preferred_element_type=f32)


def mm_nt(a, b):
    return lax.dot_general(a, b, CONTRACT_COLS, preferred_element_type=f32)


def mm_tn(a, b):
    return lax.dot_general(a, b, CONTRACT_ROWS, preferred_element_type=f32)


def feature_tables(heads):
    e1 = np.zeros((FK, LANES), np.float32)
    e2 = np.zeros((FK, LANES), np.float32)
    weight = np.zeros((LANES,), np.float32)
    bias = np.zeros((8, LANES), np.float32)
    bias[0, 0] = bias[1, 0] = weight[0] = 1.0
    for i in range(FK):
        e1[i, 1 + i] = 1.0
        bias[1, 1 + i] = 1.0
        weight[1 + i] = FK ** -0.5
    column = 1 + FK
    for i in range(FK):
        for j in range(i, FK):
            e1[i, column] = 1.0
            e2[j, column] = 1.0
            weight[column] = 1.0 / FK if i < j else 0.5 / FK
            column += 1
    def spread(table):
        out = np.zeros((heads, FK, heads, LANES), np.float32)
        for h in range(heads):
            out[h, :, h] = table
        return jnp.asarray(out.reshape(heads * FK, heads * LANES), bf16)
    return spread(e1), spread(e1 * weight), spread(e2), jnp.asarray(bias)


def features(rows, e1_ref, e2_ref, bias_ref, head):
    cols = slice(head * LANES, (head + 1) * LANES)
    first = mm(rows, e1_ref[:, cols]) + bias_ref[0:1, :]
    second = mm(rows, e2_ref[:, cols]) + bias_ref[1:2, :]
    return first, second


def features_pull(grad, first, second, e1_ref, e2_ref, head):
    cols = slice(head * LANES, (head + 1) * LANES)
    return mm_nt((grad * second).astype(bf16), e1_ref[:, cols]) + mm_nt(
        (grad * first).astype(bf16), e2_ref[:, cols]
    )


def head_only(rows, head, scale):
    lane = lax.broadcasted_iota(jnp.int32, rows.shape, 1)
    keep = (lane >= head * FK) & (lane < (head + 1) * FK)
    return jnp.where(keep, rows.astype(f32) * scale, 0.0).astype(bf16)


def full_state(state):
    return jnp.concatenate(
        [state.astype(bf16), jnp.zeros((LANES - STATE_ROWS, VD), bf16)], axis=0
    )


def conv_kernel(heads, parts, *refs):
    place_ref = refs[0]
    pieces = refs[1 : 1 + parts]
    halo_ref, taps_ref, e1_ref, e2_ref, bias_ref = refs[1 + parts : 6 + parts]
    q_ref, k_ref, v_ref, mixed_ref, state_ref, total_ref = refs[6 + parts : 12 + parts]
    piece_scr, prev_scr, total_scr = refs[12 + parts :]
    chunk = pl.program_id(0)
    relative = chunk ^ place_ref[0]
    for j in range(parts):
        @pl.when(relative == j)
        def _(j=j):
            piece_scr[...] = pieces[j][...]

    @pl.when(chunk == 0)
    def _():
        prev_scr[...] = halo_ref[...].astype(f32)
        total_scr[...] = jnp.zeros_like(total_scr)

    vw = heads * VD
    kw = heads * FK
    values = piece_scr[:, :vw]
    q = piece_scr[:, vw : vw + kw]
    k = piece_scr[:, vw + kw : vw + 2 * kw]
    q_ref[...] = q
    k_ref[...] = k
    v_ref[...] = values
    wide = values.astype(f32)
    rows = wide.shape[0]
    at = lax.broadcasted_iota(jnp.int32, wide.shape, 0)
    before1 = prev_scr[7:8, :]
    before2 = prev_scr[6:7, :]
    lag1 = jnp.where(at == 0, before1, pltpu.roll(wide, 1, 0))
    lag2 = jnp.where(at == 0, before2, jnp.where(at == 1, before1, pltpu.roll(wide, 2, 0)))
    prev_scr[...] = wide[rows - 8 :, :]
    mixed = (taps_ref[0:1, :] * wide + taps_ref[1:2, :] * lag1 + taps_ref[2:3, :] * lag2).astype(
        bf16
    )
    mixed_ref[...] = mixed
    for h in range(heads):
        first, second = features(k, e1_ref, e2_ref, bias_ref, h)
        phi = (first * second).astype(bf16)
        state = mm_tn(phi, mixed[:, h * VD : (h + 1) * VD])[:STATE_ROWS]
        state_ref[0, h] = state.astype(bf16)
        total_scr[h] += state

    @pl.when(chunk == pl.num_programs(0) - 1)
    def _():
        total_ref[...] = total_scr[...].astype(bf16)


def attend_kernel(heads, *refs):
    (
        place_ref, q_ref, k_ref, mixed_ref, state_ref, carried_ref, ga_ref, gain_ref,
        e1q_ref, e1k_ref, e2_ref, bias_ref,
        attn_ref, gq_ref, dk_ref, dv_ref, gstate_ref, gtotal_ref, gain_sum_ref, halo_ref,
        run_scr, gtotal_scr,
    ) = refs
    chunk = pl.program_id(0)

    @pl.when(chunk == 0)
    def _():
        run_scr[...] = carried_ref[...].astype(f32)
        gtotal_scr[...] = jnp.zeros_like(gtotal_scr)
        gain_sum_ref[...] = jnp.zeros_like(gain_sum_ref)

    q = q_ref[...]
    k = k_ref[...]
    rows = q.shape[0]
    row = lax.broadcasted_iota(jnp.int32, (rows, rows), 0)
    col = lax.broadcasted_iota(jnp.int32, (rows, rows), 1)
    causal = row >= col
    dq = jnp.zeros(q.shape, f32)
    dk = jnp.zeros(q.shape, f32)
    for h in range(heads):
        lanes = slice(h * VD, (h + 1) * VD)
        v = mixed_ref[:, lanes]
        first, second = features(q, e1q_ref, e2_ref, bias_ref, h)
        phi = (first * second).astype(bf16)
        state = full_state(run_scr[h])
        kh = head_only(k, h, FK ** -0.5)
        qh = head_only(q, h, FK ** -0.5)
        u = mm_nt(q, kh)
        weight = jnp.where(causal, 1.0 + u + 0.5 * u * u, 0.0).astype(bf16)
        summed = mm(weight, v) + mm(phi, state)
        scale = lax.rsqrt(jnp.mean(summed * summed, axis=-1, keepdims=True) + EPS)
        unit = summed * scale
        gain = gain_ref[0:1, lanes]
        attn_ref[0, :, lanes] = (unit * gain).astype(bf16)
        ga = ga_ref[0, :, lanes].astype(f32)
        gu = ga * unit
        gain_sum_ref[0:1, lanes] += jnp.sum(gu, axis=0, keepdims=True)
        ds = scale * (ga * gain - unit * jnp.mean(gu * gain, axis=-1, keepdims=True))
        ds = ds.astype(bf16)
        dw = mm_nt(ds, v).astype(bf16).astype(f32)
        du = jnp.where(causal, dw * (1.0 + u), 0.0).astype(bf16)
        dq += mm(du, kh)
        dk += mm_tn(du, qh)
        dv_ref[:, lanes] = mm_tn(weight, ds).astype(bf16)
        gstate = mm_tn(phi, ds)[:STATE_ROWS]
        gstate_ref[0, h] = gstate.astype(bf16)
        gtotal_scr[h] += gstate
        dphi = mm_nt(ds, state)
        dq += features_pull(dphi, first, second, e1q_ref, e2_ref, h)
        run_scr[h] += state_ref[0, h].astype(f32)

        @pl.when(chunk == 0)
        def _(h=h, lanes=lanes, gstate=gstate):
            kfirst, ksecond = features(k[0:16, :], e1k_ref, e2_ref, bias_ref, h)
            kphi = (kfirst * ksecond).astype(bf16)
            own = mm(kphi, full_state(gstate))
            halo_ref[:, lanes] = (dv_ref[0:16, lanes].astype(f32) - own)[0:8]

    gq_ref[...] = dq.astype(bf16)
    dk_ref[...] = dk

    @pl.when(chunk == pl.num_programs(0) - 1)
    def _():
        gtotal_ref[...] = gtotal_scr[...].astype(bf16)


def finish_kernel(heads, *refs):
    (
        place_ref, q_grad_ref, k_ref, v_ref, mixed_ref, dk_ref, dv_ref, gstate_ref, gin_ref,
        taps_ref, hk_ref, hv_ref, gain_ref, e1_ref, e2_ref, bias_ref,
        cols_ref, sums_ref,
        run_scr, next_scr, mixed_scr,
    ) = refs
    step = pl.program_id(0)

    @pl.when(step == 0)
    def _():
        run_scr[...] = gin_ref[...].astype(f32)
        sums_ref[...] = jnp.zeros_like(sums_ref)
        sums_ref[3:4, :] = gain_ref[0:1, :]
        hk = hk_ref[...]
        for h in range(heads):
            lanes = slice(h * VD, (h + 1) * VD)
            first, second = features(hk, e1_ref, e2_ref, bias_ref, h)
            phi = (first * second).astype(bf16)
            next_scr[:, lanes] = hv_ref[:, lanes] + mm(phi, full_state(gin_ref[h]))[0:8]

    k = k_ref[...]
    dk = dk_ref[...]
    for h in range(heads):
        lanes = slice(h * VD, (h + 1) * VD)
        first, second = features(k, e1_ref, e2_ref, bias_ref, h)
        phi = (first * second).astype(bf16)
        state = full_state(run_scr[h])
        mixed_scr[:, lanes] = dv_ref[:, lanes].astype(f32) + mm(phi, state)
        dphi = mm_nt(mixed_ref[:, lanes], state)
        dk += features_pull(dphi, first, second, e1_ref, e2_ref, h)
        run_scr[h] += gstate_ref[0, h].astype(f32)
    gm = mixed_scr[...]
    rows = gm.shape[0]
    at = lax.broadcasted_iota(jnp.int32, gm.shape, 0)
    after0 = next_scr[0:1, :]
    after1 = next_scr[1:2, :]
    lead1 = jnp.where(at == rows - 1, after0, pltpu.roll(gm, rows - 1, 0))
    lead2 = jnp.where(
        at == rows - 1, after1, jnp.where(at == rows - 2, after0, pltpu.roll(gm, rows - 2, 0))
    )
    next_scr[...] = gm[0:8, :]
    gv = taps_ref[0:1, :] * gm + taps_ref[1:2, :] * lead1 + taps_ref[2:3, :] * lead2
    values = v_ref[...].astype(f32)
    sums_ref[0:1, :] += jnp.sum(gm * values, axis=0, keepdims=True)
    sums_ref[1:2, :] += jnp.sum(lead1 * values, axis=0, keepdims=True)
    sums_ref[2:3, :] += jnp.sum(lead2 * values, axis=0, keepdims=True)
    vw = heads * VD
    kw = heads * FK
    cols_ref[0, :, :vw] = gv.astype(bf16)
    cols_ref[0, :, vw : vw + kw] = q_grad_ref[...]
    cols_ref[0, :, vw + kw :] = dk.astype(bf16)


def whole(shape):
    return pl.BlockSpec(shape, lambda *a, n=len(shape): (0,) * n)


def call(kernel, place, inputs, in_specs, out_shapes, out_specs, scratch, steps, flops):
    moved = sum(int(np.prod(x.shape)) * x.dtype.itemsize for x in inputs) + sum(
        int(np.prod(x.shape)) * x.dtype.itemsize for x in out_shapes
    )
    return pl.pallas_call(
        kernel,
        out_shape=out_shapes,
        grid_spec=pltpu.PrefetchScalarGridSpec(
            num_scalar_prefetch=1,
            grid=(steps,),
            in_specs=in_specs,
            out_specs=out_specs,
            scratch_shapes=scratch,
        ),
        compiler_params=pltpu.CompilerParams(
            dimension_semantics=("arbitrary",), vmem_limit_bytes=48 << 20
        ),
        cost_estimate=pl.CostEstimate(flops=flops, bytes_accessed=moved, transcendentals=0),
    )(place, *inputs)


def flip(x, axis, mask):
    n = lax.axis_size(axis)
    return lax.ppermute(x, axis, [(i, i ^ mask) for i in range(n)])


def gathered(x, after=None):
    n = lax.axis_size("tensor")
    if after is not None:
        x, _ = lax.optimization_barrier((x, after))
    pieces = [x, flip(x, "tensor", 1)]
    for j in range(2, n, 2):
        far = flip(x, "tensor", j)
        pieces += [far, flip(far, "tensor", 1)]
    return pieces


def scattered(partial_of):
    n = lax.axis_size("tensor")
    odd = partial_of(list(range(1, n, 2))).astype(bf16)
    got = flip(odd, "tensor", 1)
    rows = got.shape[0] // (n // 2)
    total = None
    for i, j in list(enumerate(range(0, n, 2)))[::-1]:
        part = partial_of([j]) + got[i * rows : (i + 1) * rows].astype(f32)
        if j:
            part = flip(part.astype(bf16), "tensor", j).astype(f32)
        total = part if total is None else total + part
    return total.astype(bf16)


def running(state, reverse):
    n, place = lax.axis_size("seq"), lax.axis_index("seq")
    before = jnp.zeros(state.shape, f32)
    total = state
    mask = 1
    while mask < n:
        got = flip(total.astype(bf16), "seq", mask).astype(f32)
        upper = (place & mask) != 0
        before += jnp.where(upper != reverse, got, 0.0)
        total = total.astype(f32) + got
        mask *= 2
    return before.astype(bf16)


def halved(blocks):
    n = lax.axis_size("seq")
    mask = 1
    while mask < n:
        pairs = blocks.reshape((blocks.shape[0] // 2, 2) + blocks.shape[1:])
        got = flip(pairs[:, 1], "seq", mask)
        blocks = (pairs[:, 0].astype(f32) + got.astype(f32)).astype(bf16)
        mask *= 2
    return blocks[0]


def summed_over(x, axis):
    mask = 1
    while mask < lax.axis_size(axis):
        x = x + flip(x, axis, mask)
        mask *= 2
    return x


def tn_kernel(scale, parts, relative, *refs):
    left = refs[1 : 1 + parts]
    right = refs[1 + parts : 1 + 2 * parts]
    out_ref = refs[1 + 2 * parts]
    total = mm_tn(left[0][...], right[0][...])
    for a, b in zip(left[1:], right[1:]):
        total += mm_tn(a[...], b[...])
    out_ref[0] = (total * scale).astype(bf16)


def out_blocks(attn, cotangent, scale):
    n, place = lax.axis_size("seq"), lax.axis_index("seq")
    parts, rows, vw = attn.shape
    width = cotangent[0].shape[1] // n
    if width % 128:
        full = sum(mm_tn(attn[j], cotangent[j]) for j in range(parts)) * scale
        full = full.astype(bf16).reshape(vw, n, width).transpose(1, 0, 2)
        return jnp.take(full, jnp.arange(n) ^ place, axis=0)
    return call(
        functools.partial(tn_kernel, scale, parts, True),
        place.reshape(1).astype(jnp.int32),
        [attn[j] for j in range(parts)] + list(cotangent),
        [whole((rows, vw))] * parts
        + [pl.BlockSpec((rows, width), lambda i, p: (0, i ^ p[0]))] * parts,
        [jax.ShapeDtypeStruct((n, vw, width), bf16)],
        [pl.BlockSpec((1, vw, width), lambda i, p: (i, 0, 0))],
        [], n, 2 * parts * rows * vw * width * n,
    )[0]


def in_blocks(pieces, cols, scale):
    n, place = lax.axis_size("seq"), lax.axis_index("seq")
    parts, rows, cw = cols.shape
    width = pieces[0].shape[1] // n
    if width % 128:
        full = sum(mm_tn(pieces[j], cols[j]) for j in range(parts)) * scale
        full = full.astype(bf16).reshape(n, width, cw)
        return jnp.take(full, jnp.arange(n) ^ place, axis=0)
    return call(
        functools.partial(tn_kernel, scale, parts, True),
        place.reshape(1).astype(jnp.int32),
        list(pieces) + [cols[j] for j in range(parts)],
        [pl.BlockSpec((rows, width), lambda i, p: (0, i ^ p[0]))] * parts
        + [whole((rows, cw))] * parts,
        [jax.ShapeDtypeStruct((n, width, cw), bf16)],
        [pl.BlockSpec((1, width, cw), lambda i, p: (i, 0, 0))],
        [], n, 2 * parts * rows * cw * width * n,
    )[0]


def per_device(tokens_in, w_query, w_key, w_value, w_output, conv_taps, norm_gain, grad_out):
    nt, ns = lax.axis_size("tensor"), lax.axis_size("seq")
    rows, depth = tokens_in.shape
    length = rows * nt
    kw, vw = w_query.shape[1], w_value.shape[1]
    heads = vw // VD
    grad_scale = float(length * ns) ** -0.5
    place = lax.axis_index("tensor").reshape(1).astype(jnp.int32)
    e1q, e1k, e2, bias = feature_tables(heads)

    tail = tokens_in[rows - 2 :]
    above = sum(
        lax.ppermute(
            tail, ("seq", "tensor"), [(s * nt + nt - 1, (s + 1) * nt + i) for s in range(ns - 1)]
        )
        for i in range(nt)
    )
    tokens = gathered(tokens_in)
    weights = jnp.concatenate([w_value, w_query, w_key], axis=1)
    cw = vw + 2 * kw
    projected = [mm(piece, weights).astype(bf16) for piece in tokens]
    halo = jnp.pad(mm(above, w_value).astype(bf16), ((6, 0), (0, 0)))

    state_shape = (heads, STATE_ROWS, VD)
    at_chunk = lambda i, p: (i, 0)
    at_state = lambda i, p: (i, 0, 0, 0)
    at_piece = lambda i, p: (i ^ p[0], 0, 0)
    tables = [whole(e1q.shape), whole(e2.shape), whole(bias.shape)]
    q, k, values, mixed, states, total = call(
        functools.partial(conv_kernel, heads, nt),
        place,
        projected + [halo, conv_taps, e1k, e2, bias],
        [whole((rows, cw))] * nt + [whole((8, vw)), whole((3, vw))] + tables,
        [
            jax.ShapeDtypeStruct((length, kw), bf16),
            jax.ShapeDtypeStruct((length, kw), bf16),
            jax.ShapeDtypeStruct((length, vw), bf16),
            jax.ShapeDtypeStruct((length, vw), bf16),
            jax.ShapeDtypeStruct((nt,) + state_shape, bf16),
            jax.ShapeDtypeStruct(state_shape, bf16),
        ],
        [
            pl.BlockSpec((rows, kw), at_chunk),
            pl.BlockSpec((rows, kw), at_chunk),
            pl.BlockSpec((rows, vw), at_chunk),
            pl.BlockSpec((rows, vw), at_chunk),
            pl.BlockSpec((1,) + state_shape, at_state),
            whole(state_shape),
        ],
        [
            pltpu.VMEM((rows, cw), bf16),
            pltpu.VMEM((8, vw), f32),
            pltpu.VMEM(state_shape, f32),
        ],
        nt, 2 * length * vw * 256 * 3,
    )
    carried = running(total, False)

    cotangent = gathered(grad_out, after=tokens[2])
    grad_attn = jnp.stack([mm_nt(piece, w_output).astype(bf16) for piece in cotangent])

    attn, gq, dk, dv, gstates, gtotal, gain_sum, hv = call(
        functools.partial(attend_kernel, heads),
        place,
        [q, k, mixed, states, carried, grad_attn, norm_gain.reshape(1, vw), e1q, e1k, e2, bias],
        [
            pl.BlockSpec((rows, kw), at_chunk),
            pl.BlockSpec((rows, kw), at_chunk),
            pl.BlockSpec((rows, vw), at_chunk),
            pl.BlockSpec((1,) + state_shape, at_state),
            whole(state_shape),
            pl.BlockSpec((1, rows, vw), at_piece),
            whole((1, vw)),
            whole(e1q.shape),
        ]
        + tables,
        [
            jax.ShapeDtypeStruct((nt, rows, vw), bf16),
            jax.ShapeDtypeStruct((length, kw), bf16),
            jax.ShapeDtypeStruct((length, kw), f32),
            jax.ShapeDtypeStruct((length, vw), bf16),
            jax.ShapeDtypeStruct((nt,) + state_shape, bf16),
            jax.ShapeDtypeStruct(state_shape, bf16),
            jax.ShapeDtypeStruct((8, vw), f32),
            jax.ShapeDtypeStruct((8, vw), f32),
        ],
        [
            pl.BlockSpec((1, rows, vw), at_piece),
            pl.BlockSpec((rows, kw), at_chunk),
            pl.BlockSpec((rows, kw), at_chunk),
            pl.BlockSpec((rows, vw), at_chunk),
            pl.BlockSpec((1,) + state_shape, at_state),
            whole(state_shape),
            whole((8, vw)),
            whole((8, vw)),
        ],
        [pltpu.VMEM(state_shape, f32), pltpu.VMEM(state_shape, f32)],
        nt, 2 * length * vw * 256 * 9,
    )
    gin = running(gtotal, True)
    down = [(i + 1, i) for i in range(ns - 1)]
    next_v = lax.ppermute(hv, "seq", down)
    next_k = lax.ppermute(k[0:16], "seq", down)

    layer_out = scattered(
        lambda which: mm(jnp.concatenate([attn[j] for j in which], axis=0), w_output)
    )
    grad_wo = halved(out_blocks(attn, cotangent, grad_scale))

    last = lambda i, p: (nt - 1 - i, 0)
    last_state = lambda i, p: (nt - 1 - i, 0, 0, 0)
    cols, sums = call(
        functools.partial(finish_kernel, heads),
        place,
        [gq, k, values, mixed, dk, dv, gstates, gin, conv_taps, next_k, next_v, gain_sum, e1k, e2, bias],
        [
            pl.BlockSpec((rows, kw), last),
            pl.BlockSpec((rows, kw), last),
            pl.BlockSpec((rows, vw), last),
            pl.BlockSpec((rows, vw), last),
            pl.BlockSpec((rows, kw), last),
            pl.BlockSpec((rows, vw), last),
            pl.BlockSpec((1,) + state_shape, last_state),
            whole(state_shape),
            whole((3, vw)),
            whole((16, kw)),
            whole((8, vw)),
            whole((8, vw)),
        ]
        + tables,
        [
            jax.ShapeDtypeStruct((nt, rows, cw), bf16),
            jax.ShapeDtypeStruct((8, vw), f32),
        ],
        [
            pl.BlockSpec((1, rows, cw), lambda i, p: ((nt - 1 - i) ^ p[0], 0, 0)),
            whole((8, vw)),
        ],
        [
            pltpu.VMEM(state_shape, f32),
            pltpu.VMEM((8, vw), f32),
            pltpu.VMEM((rows, vw), f32),
        ],
        nt, 2 * length * vw * 256 * 6,
    )
    grad_in = scattered(
        lambda which: mm_nt(jnp.concatenate([cols[j] for j in which], axis=0), weights)
    )
    in_share = halved(in_blocks(tokens, cols, grad_scale))
    sums = summed_over(sums, "seq") * grad_scale
    grad_wv = in_share[:, :vw]
    grad_wq = in_share[:, vw : vw + kw]
    grad_wk = in_share[:, vw + kw :]
    return (layer_out, grad_in, grad_wq, grad_wk, grad_wv, grad_wo, sums[0:3], sums[3])


def solution(mesh):
    return jax.shard_map(
        per_device,
        mesh=mesh,
        in_specs=(
            P(("seq", "tensor"), None),
            P(None, "tensor"),
            P(None, "tensor"),
            P(None, "tensor"),
            P("tensor", None),
            P(None, "tensor"),
            P("tensor"),
            P(("seq", "tensor"), None),
        ),
        out_specs=(
            P(("seq", "tensor"), None),
            P(("seq", "tensor"), None),
            P("seq", "tensor"),
            P("seq", "tensor"),
            P("seq", "tensor"),
            P("tensor", "seq"),
            P(None, "tensor"),
            P("tensor"),
        ),
        check_vma=False,
    )
```

```python
import functools

import jax
import jax.numpy as jnp
import numpy as np
from jax import lax
from jax.experimental import pallas as pl
from jax.experimental.pallas import tpu as pltpu
from jax.sharding import PartitionSpec as P

VD = 128
FK = 16
FEATS = 153
STATE_ROWS = 160
LANES = 256
EPS = 1e-6

bf16 = jnp.bfloat16
f32 = jnp.float32
CONTRACT_COLS = (((1,), (1,)), ((), ()))
CONTRACT_ROWS = (((0,), (0,)), ((), ()))


def mm(a, b):
    return jnp.dot(a, b, preferred_element_type=f32)


def mm_nt(a, b):
    return lax.dot_general(a, b, CONTRACT_COLS, preferred_element_type=f32)


def mm_tn(a, b):
    return lax.dot_general(a, b, CONTRACT_ROWS, preferred_element_type=f32)


def feature_tables(heads):
    e1 = np.zeros((FK, LANES), np.float32)
    e2 = np.zeros((FK, LANES), np.float32)
    weight = np.zeros((LANES,), np.float32)
    bias = np.zeros((8, LANES), np.float32)
    bias[0, 0] = bias[1, 0] = weight[0] = 1.0
    for i in range(FK):
        e1[i, 1 + i] = 1.0
        bias[1, 1 + i] = 1.0
        weight[1 + i] = FK ** -0.5
    column = 1 + FK
    for i in range(FK):
        for j in range(i, FK):
            e1[i, column] = 1.0
            e2[j, column] = 1.0
            weight[column] = 1.0 / FK if i < j else 0.5 / FK
            column += 1
    def spread(table):
        out = np.zeros((heads, FK, heads, LANES), np.float32)
        for h in range(heads):
            out[h, :, h] = table
        return jnp.asarray(out.reshape(heads * FK, heads * LANES), bf16)
    return spread(e1), spread(e1 * weight), spread(e2), jnp.asarray(bias)


def features_t(rows, e1_ref, e2_ref, bias_ref, head):
    at = slice(head * LANES, (head + 1) * LANES)
    first = mm_nt(e1_ref[at, :], rows) + bias_ref[:, 0:1]
    second = mm_nt(e2_ref[at, :], rows) + bias_ref[:, 1:2]
    return (first * second).astype(bf16)


def features(rows, e1_ref, e2_ref, bias_ref, head):
    cols = slice(head * LANES, (head + 1) * LANES)
    first = mm(rows, e1_ref[:, cols]) + bias_ref[0:1, :]
    second = mm(rows, e2_ref[:, cols]) + bias_ref[1:2, :]
    return first, second


def features_pull(grad, first, second, e1_ref, e2_ref, head):
    cols = slice(head * LANES, (head + 1) * LANES)
    return mm_nt((grad * second).astype(bf16), e1_ref[:, cols]) + mm_nt(
        (grad * first).astype(bf16), e2_ref[:, cols]
    )


def head_only(rows, head, scale):
    lane = lax.broadcasted_iota(jnp.int32, rows.shape, 1)
    keep = (lane >= head * FK) & (lane < (head + 1) * FK)
    return jnp.where(keep, rows.astype(f32) * scale, 0.0).astype(bf16)


def full_state(state):
    return jnp.concatenate(
        [state.astype(bf16), jnp.zeros((LANES - STATE_ROWS, VD), bf16)], axis=0
    )


def conv_kernel(heads, group, parts, *refs):
    place_ref = refs[0]
    pieces = refs[1 : 1 + parts]
    halo_ref, taps_ref, e1_ref, e2_ref, bias_ref = refs[1 + parts : 6 + parts]
    qk_ref, v_ref, mixed_ref, state_ref, total_ref = refs[6 + parts : 11 + parts]
    piece_scr, prev_scr, total_scr = refs[11 + parts :]
    chunk = pl.program_id(0)
    relative = chunk ^ place_ref[0]
    for j in range(parts):
        @pl.when(relative == j)
        def _(j=j):
            piece_scr[...] = pieces[j][...]

    first_lane, last_lane = group[0] * VD, (group[-1] + 1) * VD

    @pl.when(chunk == 0)
    def _():
        prev_scr[...] = halo_ref[:, first_lane:last_lane].astype(f32)
        total_scr[...] = jnp.zeros_like(total_scr)

    vw = heads * VD
    kw = heads * FK
    values = piece_scr[:, first_lane:last_lane]
    qk = piece_scr[:, vw : vw + 2 * kw]
    k = qk[:, kw:]
    qk_ref[...] = qk
    v_ref[...] = values
    wide = values.astype(f32)
    rows = wide.shape[0]
    at = lax.broadcasted_iota(jnp.int32, wide.shape, 0)
    before1 = prev_scr[7:8, :]
    before2 = prev_scr[6:7, :]
    lag1 = jnp.where(at == 0, before1, pltpu.roll(wide, 1, 0))
    lag2 = jnp.where(at == 0, before2, jnp.where(at == 1, before1, pltpu.roll(wide, 2, 0)))
    prev_scr[...] = wide[rows - 8 :, :]
    taps = taps_ref[:, first_lane:last_lane]
    mixed = (taps[0:1, :] * wide + taps[1:2, :] * lag1 + taps[2:3, :] * lag2).astype(bf16)
    mixed_ref[...] = mixed
    for i, h in enumerate(group):
        phi_t = features_t(k, e1_ref, e2_ref, bias_ref, h)
        state = mm(phi_t, mixed[:, i * VD : (i + 1) * VD])[:STATE_ROWS]
        state_ref[0, i] = state.astype(bf16)
        total_scr[i] += state

    @pl.when(chunk == pl.num_programs(0) - 1)
    def _():
        total_ref[...] = total_scr[...].astype(bf16)


def pre_kernel(heads, *refs):
    (
        _, qk_ref, mixed_ref, state_ref, e1_ref, e2_ref, bias_ref, e1t_ref, e2t_ref, biast_ref,
        local_ref, phi_ref, turned_ref, weight_ref, slope_ref, prefix_ref,
        run_scr,
    ) = refs

    @pl.when(pl.program_id(0) == 0)
    def _():
        run_scr[...] = jnp.zeros_like(run_scr)

    kw = heads * FK
    q = qk_ref[:, :kw]
    k = qk_ref[:, kw:]
    rows = q.shape[0]
    row = lax.broadcasted_iota(jnp.int32, (rows, rows), 0)
    col = lax.broadcasted_iota(jnp.int32, (rows, rows), 1)
    causal = row >= col
    for h in range(heads):
        lanes = slice(h * VD, (h + 1) * VD)
        first, second = features(q, e1_ref, e2_ref, bias_ref, h)
        phi = (first * second).astype(bf16)
        phi_ref[:, h * LANES : (h + 1) * LANES] = phi
        turned_ref[h] = features_t(q, e1t_ref, e2t_ref, biast_ref, h)
        u = mm_nt(q, head_only(k, h, FK ** -0.5))
        slope = 1.0 + u
        weight = jnp.where(causal, slope + 0.5 * u * u, 0.0).astype(bf16)
        weight_ref[h] = weight
        slope_ref[h] = jnp.where(causal, slope, 0.0).astype(bf16)
        prefix = run_scr[h].astype(bf16)
        prefix_ref[0, h] = prefix
        local = mm(weight, mixed_ref[:, lanes]) + mm(phi, full_state(prefix))
        local_ref[:, lanes] = local.astype(bf16)
        run_scr[h] += state_ref[0, h].astype(f32)


def mid_kernel(heads, parts, *refs):
    (
        place_ref, local_ref, phi_ref, turned_ref, carried_ref, ga_ref, gain_ref,
        qk_ref, weight_ref, e1k_ref, e2_ref, bias_ref,
        even_ref, odd_ref, ds_ref, gstate_ref, gtotal_ref, gain_sum_ref, halo_ref,
        gtotal_scr, attn_scr,
    ) = refs
    chunk = pl.program_id(0)
    relative = chunk ^ place_ref[0]

    @pl.when(chunk == 0)
    def _():
        gtotal_scr[...] = jnp.zeros_like(gtotal_scr)
        gain_sum_ref[...] = jnp.zeros_like(gain_sum_ref)

    for h in range(heads):
        lanes = slice(h * VD, (h + 1) * VD)
        phi = phi_ref[:, h * LANES : (h + 1) * LANES]
        summed = local_ref[:, lanes].astype(f32) + mm(phi, full_state(carried_ref[h]))
        scale = lax.rsqrt(jnp.mean(summed * summed, axis=-1, keepdims=True) + EPS)
        unit = summed * scale
        gain = gain_ref[0:1, lanes]
        attn_scr[:, lanes] = (unit * gain).astype(bf16)
        ga = ga_ref[0, :, lanes].astype(f32)
        gu = ga * unit
        gain_sum_ref[0:1, lanes] += jnp.sum(gu, axis=0, keepdims=True)
        ds = scale * (ga * gain - unit * jnp.mean(gu * gain, axis=-1, keepdims=True))
        ds = ds.astype(bf16)
        ds_ref[:, lanes] = ds
        gstate = mm(turned_ref[h], ds)[:STATE_ROWS]
        gstate_ref[0, h] = gstate.astype(bf16)
        gtotal_scr[h] += gstate

    @pl.when(chunk == 0)
    def _():
        kw = heads * FK
        vw = heads * VD
        qk = qk_ref[...]
        for h in range(heads):
            lanes = slice(h * VD, (h + 1) * VD)
            kfirst, ksecond = features(qk[:, kw:], e1k_ref, e2_ref, bias_ref, h)
            kphi = (kfirst * ksecond).astype(bf16)
            own = mm(kphi, full_state(gstate_ref[0, h]))
            top = mm_tn(weight_ref[h], ds_ref[:, lanes])
            halo_ref[:, lanes] = top[0:8] - own[0:8]
        halo_ref[:, vw:] = qk[0:8, :].astype(f32)

    @pl.when(relative % 2 == 0)
    def _():
        even_ref[relative // 2] = attn_scr[...]

    @pl.when(relative % 2 == 1)
    def _():
        odd_ref[relative // 2] = attn_scr[...]

    @pl.when(chunk == pl.num_programs(0) - 1)
    def _():
        gtotal_ref[...] = gtotal_scr[...].astype(bf16)


def post_kernel(heads, *refs):
    (
        _, qk_ref, mixed_ref, ds_ref, weight_ref, slope_ref, prefix_ref, carried_ref,
        e1q_ref, e2_ref, bias_ref,
        dqk_ref, dv_ref,
    ) = refs
    kw = heads * FK
    qk = qk_ref[...]
    q = qk[:, :kw]
    k = qk[:, kw:]
    dq = jnp.zeros(q.shape, f32)
    dk = jnp.zeros(q.shape, f32)
    for h in range(heads):
        lanes = slice(h * VD, (h + 1) * VD)
        ds = ds_ref[:, lanes]
        dw = mm_nt(ds, mixed_ref[:, lanes]).astype(bf16).astype(f32)
        du = (dw * slope_ref[h].astype(f32)).astype(bf16)
        dq += mm(du, head_only(k, h, FK ** -0.5))
        dk += mm_tn(du, head_only(q, h, FK ** -0.5))
        dv_ref[:, lanes] = mm_tn(weight_ref[h], ds).astype(bf16)
        state = full_state(prefix_ref[0, h].astype(f32) + carried_ref[h].astype(f32))
        first, second = features(q, e1q_ref, e2_ref, bias_ref, h)
        dq += features_pull(mm_nt(ds, state), first, second, e1q_ref, e2_ref, h)
    dqk_ref[:, :kw] = dq
    dqk_ref[:, kw:] = dk


def finish_kernel(heads, cut, parts, *refs):
    (
        place_ref, dqk_ref, qk_ref, v_ref, mixed_ref, dv_ref, gstate_ref, gin_ref,
        taps_ref, halo_ref, gain_ref, e1_ref, e2_ref, bias_ref,
        early_ref, late_ref, even_ref, odd_ref, sums_ref,
        run_scr, next_scr, mixed_scr, cols_scr,
    ) = refs
    step = pl.program_id(0)
    chunk = pl.num_programs(0) - 1 - step
    relative = chunk ^ place_ref[0]
    kw = heads * FK
    vw = heads * VD

    @pl.when(step == 0)
    def _():
        run_scr[...] = gin_ref[...].astype(f32)
        sums_ref[...] = jnp.zeros_like(sums_ref)
        sums_ref[3:4, :] = gain_ref[0:1, :]
        hk = jnp.concatenate([halo_ref[:, vw + kw :]] * 2, axis=0).astype(bf16)
        for h in range(heads):
            lanes = slice(h * VD, (h + 1) * VD)
            first, second = features(hk, e1_ref, e2_ref, bias_ref, h)
            phi = (first * second).astype(bf16)
            next_scr[:, lanes] = halo_ref[:, lanes] + mm(phi, full_state(gin_ref[h]))[0:8]

    k = qk_ref[:, kw:]
    dk = dqk_ref[:, kw:]
    for h in range(heads):
        lanes = slice(h * VD, (h + 1) * VD)
        first, second = features(k, e1_ref, e2_ref, bias_ref, h)
        phi = (first * second).astype(bf16)
        state = full_state(run_scr[h])
        mixed_scr[:, lanes] = dv_ref[:, lanes].astype(f32) + mm(phi, state)
        dphi = mm_nt(mixed_ref[:, lanes], state)
        dk += features_pull(dphi, first, second, e1_ref, e2_ref, h)
        run_scr[h] += gstate_ref[0, h].astype(f32)
    gm = mixed_scr[...]
    rows = gm.shape[0]
    at = lax.broadcasted_iota(jnp.int32, gm.shape, 0)
    after0 = next_scr[0:1, :]
    after1 = next_scr[1:2, :]
    lead1 = jnp.where(at == rows - 1, after0, pltpu.roll(gm, rows - 1, 0))
    lead2 = jnp.where(
        at == rows - 1, after1, jnp.where(at == rows - 2, after0, pltpu.roll(gm, rows - 2, 0))
    )
    next_scr[...] = gm[0:8, :]
    gv = taps_ref[0:1, :] * gm + taps_ref[1:2, :] * lead1 + taps_ref[2:3, :] * lead2
    values = v_ref[...].astype(f32)
    sums_ref[0:1, :] += jnp.sum(gm * values, axis=0, keepdims=True)
    sums_ref[1:2, :] += jnp.sum(lead1 * values, axis=0, keepdims=True)
    sums_ref[2:3, :] += jnp.sum(lead2 * values, axis=0, keepdims=True)
    cols_scr[:, :vw] = gv.astype(bf16)
    cols_scr[:, vw : vw + kw] = dqk_ref[:, :kw].astype(bf16)
    cols_scr[:, vw + kw :] = dk.astype(bf16)
    at_piece = relative // 2 + (relative % 2) * (parts // 2)
    early_ref[at_piece] = cols_scr[:, :cut]
    late_ref[at_piece] = cols_scr[:, cut:]

    @pl.when(relative % 2 == 0)
    def _():
        even_ref[relative // 2] = cols_scr[...]

    @pl.when(relative % 2 == 1)
    def _():
        odd_ref[relative // 2] = cols_scr[...]


def whole(shape):
    return pl.BlockSpec(shape, lambda *a, n=len(shape): (0,) * n)


def call(kernel, place, inputs, in_specs, out_shapes, out_specs, scratch, steps, flops, alias=None):
    return pl.pallas_call(
        kernel,
        out_shape=out_shapes,
        grid_spec=pltpu.PrefetchScalarGridSpec(
            num_scalar_prefetch=1,
            grid=(steps,),
            in_specs=in_specs,
            out_specs=out_specs,
            scratch_shapes=scratch,
        ),
        input_output_aliases=alias or {},
        compiler_params=pltpu.CompilerParams(
            dimension_semantics=("arbitrary",), vmem_limit_bytes=16 << 20
        ),
        cost_estimate=pl.CostEstimate(flops=0, bytes_accessed=0, transcendentals=0),
    )(place, *inputs)


def in_hbm(x):
    return pltpu.with_memory_space_constraint(x, pltpu.HBM)


def flip(x, axis, mask):
    n = lax.axis_size(axis)
    return lax.ppermute(x, axis, [(i, i ^ mask) for i in range(n)])


def held(x, *others):
    return lax.optimization_barrier((x,) + others)[0]


def scan_send(total, mask):
    return flip(total.astype(bf16), "seq", mask) if mask < lax.axis_size("seq") else None


def scan_take(before, total, got, mask, reverse):
    got = got.astype(f32)
    upper = (lax.axis_index("seq") & mask) != 0
    return before + jnp.where(upper != reverse, got, 0.0), total.astype(f32) + got


def arrange_kernel(parts, *refs):
    pieces = refs[1 : 1 + parts]
    kept_ref, sent_ref = refs[1 + parts :]
    rows = pieces[0].shape[0]
    step = pl.program_id(0)
    half = pl.num_programs(0) // 2
    for target, on in ((kept_ref, step < half), (sent_ref, step >= half)):
        @pl.when(on)
        def _(target=target):
            for j in range(parts):
                target[j * rows : (j + 1) * rows, :] = pieces[j][...]


def arranged(pieces, masks):
    n, place = lax.axis_size("seq"), lax.axis_index("seq")
    order = [0]
    for mask in masks[::-1]:
        order = order + [j | mask for j in order]
    order = jnp.asarray(np.array(order, np.int32)) ^ place.astype(jnp.int32)
    parts = len(pieces)
    rows, depth = pieces[0].shape
    length, width, half = parts * rows, depth // n, depth // 2
    if width % 128:
        full = jnp.concatenate(pieces, axis=0).reshape(length, n, width)
        full = jnp.take(full, order, axis=1).reshape(length, depth)
        return full[:, :half], full[:, half:]
    out = pltpu.HBM((length, half), bf16)
    mid = n // 2
    return call(
        functools.partial(arrange_kernel, parts),
        order,
        list(pieces),
        [pl.BlockSpec((rows, width), lambda i, o: (0, o[i]))] * parts,
        [out, out],
        [
            pl.BlockSpec((length, width), lambda i, o: (0, jnp.minimum(i, mid - 1))),
            pl.BlockSpec((length, width), lambda i, o: (0, jnp.maximum(i - mid, 0))),
        ],
        [], n, 0,
    )


class Halve:
    def __init__(self, turn, left, right, scale, extra=None):
        n = lax.axis_size("seq")
        self.masks = [1 << b for b in range(n.bit_length() - 1)]
        self.turn = turn and n > 2
        if self.turn:
            self.masks = self.masks[1:] + self.masks[:1]
        self.left, self.right, self.scale, self.extra = left, right, scale, extra

    def product(self, side, *others):
        left = held(self.left, *others) if others else self.left
        n = lax.axis_size("seq")
        width = 2 * self.right[0].shape[1] // n
        if self.turn:
            half = self.right[0].shape[1] // 2
            pair = [
                (mm_tn(left, right[:, side * half : (side + 1) * half]) * self.scale).astype(bf16)
                for right in self.right
            ]
            out = jnp.concatenate(
                [p[:, i * width : (i + 1) * width] for i in range(n // 4) for p in pair], axis=1
            )
        else:
            out = (mm_tn(left, self.right[side]) * self.scale).astype(bf16)
        if self.extra is not None:
            tail = (self.extra[:4] * self.scale).astype(bf16).reshape(4, -1, width)
            tail = tail.transpose(1, 0, 2).reshape(-1, width)
            out = jnp.concatenate([out, jnp.tile(tail, (1, n // 2))], axis=0)
        return out

    def begin(self, *others):
        self.first = self.product(1, *others)
        self.got = flip(self.first, "seq", self.masks[0])
        self.at = 1

    def keep(self, *others):
        self.kept = [self.product(0, *others)]
        return self.kept[0]

    def step(self, *others):
        got = held(self.got, *others)
        self.kept.append(got)
        if self.at == len(self.masks):
            self.out = sum(t.astype(f32) for t in self.kept)
            return self.out
        half = got.shape[1] // 2
        send = sum(t[:, half:].astype(f32) for t in self.kept).astype(bf16)
        self.got = flip(send, "seq", self.masks[self.at])
        self.at += 1
        self.kept = [t[:, :half] for t in self.kept]
        return send


def masks_of(first):
    n = lax.axis_size("seq")
    masks = [1 << b for b in range(n.bit_length() - 1)]
    return masks[first:] + masks[:first]


def per_device(tokens_in, w_query, w_key, w_value, w_output, conv_taps, norm_gain, grad_out):
    nt, ns = lax.axis_size("tensor"), lax.axis_size("seq")
    rows, depth = tokens_in.shape
    length = rows * nt
    kw, vw = w_query.shape[1], w_value.shape[1]
    heads = vw // VD
    grad_scale = float(length * ns) ** -0.5
    place = lax.axis_index("tensor").reshape(1).astype(jnp.int32)
    e1q, e1k, e2, bias = feature_tables(heads)
    turned_q, turned_k, turned2 = e1q.T, e1k.T, e2.T
    turned_bias = jnp.pad(bias[:2].T, ((0, 0), (0, 126)))
    (
        e1q, e1k, e2, bias, turned_q, turned_k, turned2, turned_bias, conv_taps, norm_gain
    ) = (
        pltpu.with_memory_space_constraint(x, pltpu.HBM)
        for x in (
            e1q, e1k, e2, bias, turned_q, turned_k, turned2, turned_bias, conv_taps,
            norm_gain.reshape(1, -1),
        )
    )
    evens, odds = list(range(0, nt, 2)), list(range(1, nt, 2))

    far = {j: flip(tokens_in, "tensor", j) for j in evens[1:]}
    near = flip(tokens_in, "tensor", 1)
    near_cot = flip(grad_out, "tensor", 1)
    tail = held(tokens_in, near)[rows - 2 :]
    above = sum(
        lax.ppermute(
            tail, ("seq", "tensor"), [(s * nt + nt - 1, (s + 1) * nt + i) for s in range(ns - 1)]
        )
        for i in range(nt)
    )
    cw = vw + 2 * kw
    joined = [held(w, near) for w in (w_value, w_query, w_key)]
    weights = lax.optimization_barrier(jnp.concatenate(joined, axis=1))
    project = lambda piece: mm(piece, weights).astype(bf16)
    pull = lambda piece: mm_nt(piece, w_output).astype(bf16)
    halo = jnp.pad(mm(above, w_value).astype(bf16), ((6, 0), (0, 0)))
    tokens, cotangent = [tokens_in, near], [grad_out, near_cot]
    projected = [project(tokens_in), project(near)]
    pulled = [pull(grad_out), pull(near_cot)]
    for j in evens[1:]:
        piece = held(far[j], halo, *projected, *pulled)
        tokens += [piece, flip(piece, "tensor", 1)]
    projected += [project(piece) for piece in tokens[2:]]
    cot_from = held(grad_out, projected[2])
    far_cot = {j: flip(cot_from, "tensor", j) for j in evens[1:]}

    state_shape = (heads, STATE_ROWS, VD)
    at_chunk = lambda i, p: (i, 0)
    at_state = lambda i, p: (i, 0, 0, 0)
    on_chunk = lambda width: pl.BlockSpec((rows, width), at_chunk)
    state_spec = pl.BlockSpec((1,) + state_shape, at_state)
    square_spec = pl.BlockSpec((heads, rows, rows), lambda i, p: (0, i, 0))
    tables = [whole(e1q.shape), whole(e2.shape), whole(bias.shape)]
    turned_tables = [whole(turned_q.shape), whole(turned2.shape), whole(turned_bias.shape)]
    turned_spec = pl.BlockSpec((heads, LANES, rows), lambda i, p: (0, 0, i))
    shape = jax.ShapeDtypeStruct
    states_shape = shape((nt,) + state_shape, bf16)
    qk, values, mixed, states, total = call(
        functools.partial(conv_kernel, heads, list(range(heads)), nt),
        place,
        projected + [halo, conv_taps, turned_k, turned2, turned_bias],
        [whole((rows, cw))] * nt + [whole((8, vw)), whole((3, vw))] + turned_tables,
        [
            shape((length, 2 * kw), bf16),
            shape((length, vw), bf16),
            shape((length, vw), bf16),
            states_shape,
            shape(state_shape, bf16),
        ],
        [on_chunk(2 * kw), on_chunk(vw), on_chunk(vw), state_spec, whole(state_shape)],
        [pltpu.VMEM((rows, cw), bf16), pltpu.VMEM((8, vw), f32), pltpu.VMEM(state_shape, f32)],
        nt, 2 * length * vw * 256 * 3,
    )

    before = jnp.zeros(state_shape, f32)
    mask = 1
    got = scan_send(total, mask)
    pinned = lambda dims, kind: pltpu.HBM(dims, kind)
    local, phi, phi_t, weight, slope, prefix = call(
        functools.partial(pre_kernel, heads),
        place,
        [qk, mixed, states, e1q, e2, bias, turned_q, turned2, turned_bias],
        [on_chunk(2 * kw), on_chunk(vw), state_spec] + tables + turned_tables,
        [
            pinned((length, vw), bf16),
            pinned((length, heads * LANES), bf16),
            pinned((heads, LANES, length), bf16),
            pinned((heads, length, rows), bf16),
            pinned((heads, length, rows), bf16),
            states_shape,
        ],
        [
            on_chunk(vw), on_chunk(heads * LANES), turned_spec, square_spec, square_spec,
            state_spec,
        ],
        [pltpu.VMEM(state_shape, f32)],
        nt, 2 * length * vw * 256 * 5,
    )
    got = held(got, local)
    ordered = lambda pieces: [pieces[j] for j in evens + odds]
    tokens_for = None
    while got is not None:
        before, total = scan_take(before, total, got, mask, False)
        mask *= 2
        got = scan_send(total, mask)
        if tokens_for is None:
            ready = ordered(tokens)
            ready[0] = held(ready[0], total)
            tokens_for = arranged(ready, masks_of(0))
            got = held(got, *tokens_for) if got is not None else None
        if mask * 2 == ns:
            for j in evens[1:]:
                piece = held(far_cot[j], total)
                cotangent += [piece, flip(piece, "tensor", 1)]
            pulled += [pull(piece) for piece in cotangent[2:]]
            by_place = [pulled[j] for j in evens + odds]
            grad_attn = jnp.stack(by_place)
            got = held(got, grad_attn)
    carried = before.astype(bf16)

    half_shape = shape((nt // 2, rows, vw), bf16)
    slot = lambda j: (j >> 1) + (j & 1) * (nt // 2)
    attn_even, attn_odd, ds, gstates, gtotal, gain_sum, halo_out = call(
        functools.partial(mid_kernel, heads, nt),
        place,
        [
            local, phi, phi_t, carried, grad_attn, norm_gain, qk, weight, e1k, e2,
            bias,
        ],
        [
            on_chunk(vw),
            on_chunk(heads * LANES),
            turned_spec,
            whole(state_shape),
            pl.BlockSpec((1, rows, vw), lambda i, p: (slot(i ^ p[0]), 0, 0)),
            whole((1, vw)),
            whole((16, 2 * kw)),
            whole((heads, rows, 128)),
        ]
        + tables,
        [
            half_shape, half_shape, shape((length, vw), bf16), states_shape,
            shape(state_shape, bf16), shape((8, vw), f32), shape((8, vw + 2 * kw), f32),
        ],
        [
            whole(half_shape.shape), whole(half_shape.shape), on_chunk(vw), state_spec,
            whole(state_shape), whole((8, vw)), whole((8, vw + 2 * kw)),
        ],
        [pltpu.VMEM(state_shape, f32), pltpu.VMEM((rows, vw), bf16)],
        nt, 2 * length * vw * 256 * 2,
    )

    attn_all = jnp.concatenate([attn_even.reshape(-1, vw), attn_odd.reshape(-1, vw)], axis=0)
    ready = ordered(cotangent)
    ready[0] = held(ready[0], gtotal)
    cot_for = arranged(ready, masks_of(0))
    out_halve = Halve(False, attn_all, cot_for, grad_scale)
    after = jnp.zeros(state_shape, f32)
    got = scan_send(gtotal, 1)
    halo_in = lax.ppermute(halo_out, "seq", [(i + 1, i) for i in range(ns - 1)])
    out_odd = mm(attn_odd.reshape(-1, vw), w_output).astype(bf16)
    out_got = flip(out_odd, "tensor", 1)
    mask = 1
    while got is not None:
        cover = [out_odd, *cot_for] if mask == 1 else [kept] if mask == 2 else [dv]
        after, gtotal = scan_take(after, gtotal, held(got, *cover), mask, True)
        mask *= 2
        got = scan_send(gtotal, mask)
        if mask == 2:
            out_flips = []
            out_rows = mm(attn_even.reshape(-1, vw), w_output) + held(out_got, gtotal).astype(f32)
            out_rows = out_rows.astype(bf16)
            for i in range(1, nt // 2):
                out_flips.append(flip(out_rows[i * rows : (i + 1) * rows], "tensor", 2 * i))
            out_halve.begin(out_rows)
            kept = out_halve.keep(out_halve.first)
        if mask == 4 or (mask == 2 and ns == 2):
            dqk, dv = call(
                functools.partial(post_kernel, heads),
                place,
                [
                    held(qk, gtotal), in_hbm(mixed), ds, in_hbm(weight), in_hbm(slope),
                    in_hbm(prefix), carried, e1q, e2, bias,
                ],
                [
                    on_chunk(2 * kw), on_chunk(vw), on_chunk(vw), square_spec, square_spec,
                    state_spec, whole(state_shape),
                ]
                + tables,
                [shape((length, 2 * kw), f32), shape((length, vw), bf16)],
                [on_chunk(2 * kw), on_chunk(vw)],
                [],
                nt, 2 * length * vw * 256 * 8,
            )
    gin = after.astype(bf16)
    dqk = held(dqk, out_halve.step(gin))

    last = lambda i, p: (nt - 1 - i, 0)
    from_last = lambda width: pl.BlockSpec((rows, width), last)
    cut = cw * 6 // 10 // 128 * 128
    early, late, cols_even, cols_odd, sums = call(
        functools.partial(finish_kernel, heads, cut, nt),
        place,
        [dqk, qk, values, mixed, dv, gstates, gin, conv_taps, halo_in, gain_sum, e1k, e2, bias],
        [
            from_last(2 * kw), from_last(2 * kw), from_last(vw), from_last(vw), from_last(vw),
            pl.BlockSpec((1,) + state_shape, lambda i, p: (nt - 1 - i, 0, 0, 0)),
            whole(state_shape), whole((3, vw)), whole((8, vw + 2 * kw)), whole((8, vw)),
        ]
        + tables,
        [
            shape((nt, rows, cut), bf16), shape((nt, rows, cw - cut), bf16),
            shape((nt // 2, rows, cw), bf16), shape((nt // 2, rows, cw), bf16),
            shape((8, vw), f32),
        ],
        [
            whole((nt, rows, cut)), whole((nt, rows, cw - cut)),
            whole((nt // 2, rows, cw)), whole((nt // 2, rows, cw)), whole((8, vw)),
        ],
        [
            pltpu.VMEM(state_shape, f32), pltpu.VMEM((8, vw), f32),
            pltpu.VMEM((rows, vw), f32), pltpu.VMEM((rows, cw), bf16),
        ],
        nt, 2 * length * vw * 256 * 6,
    )
    first = Halve(False, early.reshape(length, cut), tokens_for, grad_scale)
    out_flips = [held(got, early) for got in out_flips]
    steps = len(out_halve.masks)
    first = Halve(False, early.reshape(length, cut), tokens_for, grad_scale)
    first.begin(*out_flips)
    second = Halve(True, late.reshape(length, cw - cut), tokens_for, grad_scale, sums)
    done = out_halve.step(first.first) if steps > 2 else first.first
    second.begin(done)
    in_odd = mm_nt(held(cols_odd, second.first).reshape(-1, cw), weights).astype(bf16)
    in_got = held(flip(in_odd, "tensor", 1), in_odd)
    in_rows = mm_nt(cols_even.reshape(-1, cw), weights) + in_got.astype(f32)
    in_rows = in_rows.astype(bf16)
    in_flips = []
    for i in range(1, nt // 2):
        in_flips.append(flip(in_rows[i * rows : (i + 1) * rows], "tensor", 2 * i))
    done = first.keep(in_rows)
    done = first.step(done)
    done = second.keep(done)
    done = second.step(done)
    layer_out = held(out_rows, done)[:rows].astype(f32)
    for got in out_flips:
        layer_out += got.astype(f32)
    done = layer_out = layer_out.astype(bf16)
    for k in range(1, steps):
        if k < steps - 1 or steps == 2:
            done = out_halve.step(done)
        done = first.step(done) if k < steps - 1 else done
        done = second.step(done)
        if k == steps - 2 or steps == 2:
            grad_in = in_rows[:rows].astype(f32)
            for got in in_flips:
                grad_in += held(got, done).astype(f32)
            done = grad_in = grad_in.astype(bf16)
    first.step(done)
    while not hasattr(out_halve, "out"):
        out_halve.step(done)
    grad_wo = out_halve.out.astype(bf16)
    low, high = first.out.astype(bf16), second.out[: cw - cut].astype(bf16)
    sums = second.out[cw - cut :]
    sums = jnp.concatenate(jnp.split(sums, sums.shape[0] // 4, axis=0), axis=1)
    more = vw - cut
    grad_wv = jnp.concatenate([low.T, high[:more].T], axis=1)
    grad_wq = high[more : more + kw].T
    grad_wk = high[more + kw :].T
    return (layer_out, grad_in, grad_wq, grad_wk, grad_wv, grad_wo, sums[0:3], sums[3])


def solution(mesh):
    return jax.shard_map(
        per_device,
        mesh=mesh,
        in_specs=(
            P(("seq", "tensor"), None),
            P(None, "tensor"),
            P(None, "tensor"),
            P(None, "tensor"),
            P("tensor", None),
            P(None, "tensor"),
            P("tensor"),
            P(("seq", "tensor"), None),
        ),
        out_specs=(
            P(("seq", "tensor"), None),
            P(("seq", "tensor"), None),
            P("seq", "tensor"),
            P("seq", "tensor"),
            P("seq", "tensor"),
            P("tensor", "seq"),
            P(None, "tensor"),
            P("tensor"),
        ),
        check_vma=False,
    )
```

```python
import functools

import jax
import jax.numpy as jnp
import numpy as np
from jax import lax
from jax.experimental import pallas as pl
from jax.experimental.pallas import tpu as pltpu
from jax.sharding import PartitionSpec as P

VD = 128
FK = 16
FEATS = 153
STATE_ROWS = 160
LANES = 256
EPS = 1e-6

bf16 = jnp.bfloat16
f32 = jnp.float32
CONTRACT_COLS = (((1,), (1,)), ((), ()))
CONTRACT_ROWS = (((0,), (0,)), ((), ()))


def mm(a, b):
    return jnp.dot(a, b, preferred_element_type=f32)


def mm_nt(a, b):
    return lax.dot_general(a, b, CONTRACT_COLS, preferred_element_type=f32)


def mm_tn(a, b):
    return lax.dot_general(a, b, CONTRACT_ROWS, preferred_element_type=f32)


def feature_tables(heads):
    e1 = np.zeros((FK, LANES), np.float32)
    e2 = np.zeros((FK, LANES), np.float32)
    weight = np.zeros((LANES,), np.float32)
    bias = np.zeros((8, LANES), np.float32)
    bias[0, 0] = bias[1, 0] = weight[0] = 1.0
    for i in range(FK):
        e1[i, 1 + i] = 1.0
        bias[1, 1 + i] = 1.0
        weight[1 + i] = FK ** -0.5
    column = 1 + FK
    for i in range(FK):
        for j in range(i, FK):
            e1[i, column] = 1.0
            e2[j, column] = 1.0
            weight[column] = 1.0 / FK if i < j else 0.5 / FK
            column += 1
    def spread(table):
        out = np.zeros((heads, FK, heads, LANES), np.float32)
        for h in range(heads):
            out[h, :, h] = table
        return jnp.asarray(out.reshape(heads * FK, heads * LANES), bf16)
    return spread(e1), spread(e1 * weight), spread(e2), jnp.asarray(bias)


def features_t(rows, e1_ref, e2_ref, bias_ref, head):
    at = slice(head * LANES, (head + 1) * LANES)
    first = mm_nt(e1_ref[at, :], rows) + bias_ref[:, 0:1]
    second = mm_nt(e2_ref[at, :], rows) + bias_ref[:, 1:2]
    return (first * second).astype(bf16)


def features(rows, e1_ref, e2_ref, bias_ref, head):
    cols = slice(head * LANES, (head + 1) * LANES)
    first = mm(rows, e1_ref[:, cols]) + bias_ref[0:1, :]
    second = mm(rows, e2_ref[:, cols]) + bias_ref[1:2, :]
    return first, second


def features_pull(grad, first, second, e1_ref, e2_ref, head):
    cols = slice(head * LANES, (head + 1) * LANES)
    return mm_nt((grad * second).astype(bf16), e1_ref[:, cols]) + mm_nt(
        (grad * first).astype(bf16), e2_ref[:, cols]
    )


def head_only(rows, head, scale):
    lane = lax.broadcasted_iota(jnp.int32, rows.shape, 1)
    keep = (lane >= head * FK) & (lane < (head + 1) * FK)
    return jnp.where(keep, rows.astype(f32) * scale, 0.0).astype(bf16)


def full_state(state):
    return jnp.concatenate(
        [state.astype(bf16), jnp.zeros((LANES - STATE_ROWS, VD), bf16)], axis=0
    )


def conv_kernel(heads, group, parts, *refs):
    place_ref = refs[0]
    pieces = refs[1 : 1 + parts]
    halo_ref, taps_ref, e1_ref, e2_ref, bias_ref = refs[1 + parts : 6 + parts]
    qk_ref, v_ref, mixed_ref, state_ref, total_ref = refs[6 + parts : 11 + parts]
    piece_scr, prev_scr, total_scr = refs[11 + parts :]
    chunk = pl.program_id(0)
    relative = chunk ^ place_ref[0]
    for j in range(parts):
        @pl.when(relative == j)
        def _(j=j):
            piece_scr[...] = pieces[j][...]

    first_lane, last_lane = group[0] * VD, (group[-1] + 1) * VD

    @pl.when(chunk == 0)
    def _():
        prev_scr[...] = halo_ref[:, first_lane:last_lane].astype(f32)
        total_scr[...] = jnp.zeros_like(total_scr)

    vw = heads * VD
    kw = heads * FK
    values = piece_scr[:, first_lane:last_lane]
    qk = piece_scr[:, vw : vw + 2 * kw]
    k = qk[:, kw:]
    qk_ref[...] = qk
    v_ref[...] = values
    wide = values.astype(f32)
    rows = wide.shape[0]
    at = lax.broadcasted_iota(jnp.int32, wide.shape, 0)
    before1 = prev_scr[7:8, :]
    before2 = prev_scr[6:7, :]
    lag1 = jnp.where(at == 0, before1, pltpu.roll(wide, 1, 0))
    lag2 = jnp.where(at == 0, before2, jnp.where(at == 1, before1, pltpu.roll(wide, 2, 0)))
    prev_scr[...] = wide[rows - 8 :, :]
    taps = taps_ref[:, first_lane:last_lane]
    mixed = (taps[0:1, :] * wide + taps[1:2, :] * lag1 + taps[2:3, :] * lag2).astype(bf16)
    mixed_ref[...] = mixed
    for i, h in enumerate(group):
        phi_t = features_t(k, e1_ref, e2_ref, bias_ref, h)
        state = mm(phi_t, mixed[:, i * VD : (i + 1) * VD])[:STATE_ROWS]
        state_ref[0, i] = state.astype(bf16)
        total_scr[i] += state

    @pl.when(chunk == pl.num_programs(0) - 1)
    def _():
        total_ref[...] = total_scr[...].astype(bf16)


def pre_kernel(heads, *refs):
    (
        _, qk_ref, mixed_ref, state_ref, e1_ref, e2_ref, bias_ref, e1t_ref, e2t_ref, biast_ref,
        local_ref, phi_ref, turned_ref, weight_ref, slope_ref, prefix_ref,
        run_scr,
    ) = refs

    @pl.when(pl.program_id(0) == 0)
    def _():
        run_scr[...] = jnp.zeros_like(run_scr)

    kw = heads * FK
    q = qk_ref[:, :kw]
    k = qk_ref[:, kw:]
    rows = q.shape[0]
    row = lax.broadcasted_iota(jnp.int32, (rows, rows), 0)
    col = lax.broadcasted_iota(jnp.int32, (rows, rows), 1)
    causal = row >= col
    for h in range(heads):
        lanes = slice(h * VD, (h + 1) * VD)
        first, second = features(q, e1_ref, e2_ref, bias_ref, h)
        phi = (first * second).astype(bf16)
        phi_ref[:, h * LANES : (h + 1) * LANES] = phi
        turned_ref[h] = features_t(q, e1t_ref, e2t_ref, biast_ref, h)
        u = mm_nt(q, head_only(k, h, FK ** -0.5))
        slope = 1.0 + u
        weight = jnp.where(causal, slope + 0.5 * u * u, 0.0).astype(bf16)
        weight_ref[h] = weight
        slope_ref[h] = jnp.where(causal, slope, 0.0).astype(bf16)
        prefix = run_scr[h].astype(bf16)
        prefix_ref[0, h] = prefix
        local = mm(weight, mixed_ref[:, lanes]) + mm(phi, full_state(prefix))
        local_ref[:, lanes] = local.astype(bf16)
        run_scr[h] += state_ref[0, h].astype(f32)


def mid_kernel(heads, parts, *refs):
    (
        place_ref, local_ref, phi_ref, turned_ref, carried_ref, ga_ref, gain_ref,
        qk_ref, weight_ref, e1k_ref, e2_ref, bias_ref,
        even_ref, odd_ref, ds_ref, gstate_ref, gtotal_ref, gain_sum_ref, halo_ref,
        gtotal_scr, attn_scr,
    ) = refs
    chunk = pl.program_id(0)
    relative = chunk ^ place_ref[0]

    @pl.when(chunk == 0)
    def _():
        gtotal_scr[...] = jnp.zeros_like(gtotal_scr)
        gain_sum_ref[...] = jnp.zeros_like(gain_sum_ref)

    for h in range(heads):
        lanes = slice(h * VD, (h + 1) * VD)
        phi = phi_ref[:, h * LANES : (h + 1) * LANES]
        summed = local_ref[:, lanes].astype(f32) + mm(phi, full_state(carried_ref[h]))
        scale = lax.rsqrt(jnp.mean(summed * summed, axis=-1, keepdims=True) + EPS)
        unit = summed * scale
        gain = gain_ref[0:1, lanes]
        attn_scr[:, lanes] = (unit * gain).astype(bf16)
        ga = ga_ref[0, :, lanes].astype(f32)
        gu = ga * unit
        gain_sum_ref[0:1, lanes] += jnp.sum(gu, axis=0, keepdims=True)
        ds = scale * (ga * gain - unit * jnp.mean(gu * gain, axis=-1, keepdims=True))
        ds = ds.astype(bf16)
        ds_ref[:, lanes] = ds
        gstate = mm(turned_ref[h], ds)[:STATE_ROWS]
        gstate_ref[0, h] = gstate.astype(bf16)
        gtotal_scr[h] += gstate

    @pl.when(chunk == 0)
    def _():
        kw = heads * FK
        vw = heads * VD
        qk = qk_ref[...]
        for h in range(heads):
            lanes = slice(h * VD, (h + 1) * VD)
            kfirst, ksecond = features(qk[:, kw:], e1k_ref, e2_ref, bias_ref, h)
            kphi = (kfirst * ksecond).astype(bf16)
            own = mm(kphi, full_state(gstate_ref[0, h]))
            top = mm_tn(weight_ref[h], ds_ref[:, lanes])
            halo_ref[:, lanes] = top[0:8] - own[0:8]
        halo_ref[:, vw:] = qk[0:8, :].astype(f32)

    @pl.when(relative % 2 == 0)
    def _():
        even_ref[relative // 2] = attn_scr[...]

    @pl.when(relative % 2 == 1)
    def _():
        odd_ref[relative // 2] = attn_scr[...]

    @pl.when(chunk == pl.num_programs(0) - 1)
    def _():
        gtotal_ref[...] = gtotal_scr[...].astype(bf16)


def post_kernel(heads, *refs):
    (
        _, qk_ref, mixed_ref, ds_ref, weight_ref, slope_ref, prefix_ref, carried_ref,
        e1q_ref, e2_ref, bias_ref,
        dqk_ref, dv_ref,
    ) = refs
    kw = heads * FK
    qk = qk_ref[...]
    q = qk[:, :kw]
    k = qk[:, kw:]
    dq = jnp.zeros(q.shape, f32)
    dk = jnp.zeros(q.shape, f32)
    for h in range(heads):
        lanes = slice(h * VD, (h + 1) * VD)
        ds = ds_ref[:, lanes]
        dw = mm_nt(ds, mixed_ref[:, lanes]).astype(bf16).astype(f32)
        du = (dw * slope_ref[h].astype(f32)).astype(bf16)
        dq += mm(du, head_only(k, h, FK ** -0.5))
        dk += mm_tn(du, head_only(q, h, FK ** -0.5))
        dv_ref[:, lanes] = mm_tn(weight_ref[h], ds).astype(bf16)
        state = full_state(prefix_ref[0, h].astype(f32) + carried_ref[h].astype(f32))
        first, second = features(q, e1q_ref, e2_ref, bias_ref, h)
        dq += features_pull(mm_nt(ds, state), first, second, e1q_ref, e2_ref, h)
    dqk_ref[:, :kw] = dq
    dqk_ref[:, kw:] = dk


def finish_kernel(heads, cut, parts, *refs):
    (
        place_ref, dqk_ref, qk_ref, v_ref, mixed_ref, dv_ref, gstate_ref, gin_ref,
        taps_ref, halo_ref, gain_ref, e1_ref, e2_ref, bias_ref,
        early_ref, late_ref, even_ref, odd_ref, sums_ref,
        run_scr, next_scr, mixed_scr, cols_scr,
    ) = refs
    step = pl.program_id(0)
    chunk = pl.num_programs(0) - 1 - step
    relative = chunk ^ place_ref[0]
    kw = heads * FK
    vw = heads * VD

    @pl.when(step == 0)
    def _():
        run_scr[...] = gin_ref[...].astype(f32)
        sums_ref[...] = jnp.zeros_like(sums_ref)
        sums_ref[3:4, :] = gain_ref[0:1, :]
        hk = jnp.concatenate([halo_ref[:, vw + kw :]] * 2, axis=0).astype(bf16)
        for h in range(heads):
            lanes = slice(h * VD, (h + 1) * VD)
            first, second = features(hk, e1_ref, e2_ref, bias_ref, h)
            phi = (first * second).astype(bf16)
            next_scr[:, lanes] = halo_ref[:, lanes] + mm(phi, full_state(gin_ref[h]))[0:8]

    k = qk_ref[:, kw:]
    dk = dqk_ref[:, kw:]
    for h in range(heads):
        lanes = slice(h * VD, (h + 1) * VD)
        first, second = features(k, e1_ref, e2_ref, bias_ref, h)
        phi = (first * second).astype(bf16)
        state = full_state(run_scr[h])
        mixed_scr[:, lanes] = dv_ref[:, lanes].astype(f32) + mm(phi, state)
        dphi = mm_nt(mixed_ref[:, lanes], state)
        dk += features_pull(dphi, first, second, e1_ref, e2_ref, h)
        run_scr[h] += gstate_ref[0, h].astype(f32)
    gm = mixed_scr[...]
    rows = gm.shape[0]
    at = lax.broadcasted_iota(jnp.int32, gm.shape, 0)
    after0 = next_scr[0:1, :]
    after1 = next_scr[1:2, :]
    lead1 = jnp.where(at == rows - 1, after0, pltpu.roll(gm, rows - 1, 0))
    lead2 = jnp.where(
        at == rows - 1, after1, jnp.where(at == rows - 2, after0, pltpu.roll(gm, rows - 2, 0))
    )
    next_scr[...] = gm[0:8, :]
    gv = taps_ref[0:1, :] * gm + taps_ref[1:2, :] * lead1 + taps_ref[2:3, :] * lead2
    values = v_ref[...].astype(f32)
    sums_ref[0:1, :] += jnp.sum(gm * values, axis=0, keepdims=True)
    sums_ref[1:2, :] += jnp.sum(lead1 * values, axis=0, keepdims=True)
    sums_ref[2:3, :] += jnp.sum(lead2 * values, axis=0, keepdims=True)
    cols_scr[:, :vw] = gv.astype(bf16)
    cols_scr[:, vw : vw + kw] = dqk_ref[:, :kw].astype(bf16)
    cols_scr[:, vw + kw :] = dk.astype(bf16)
    at_piece = relative // 2 + (relative % 2) * (parts // 2)
    early_ref[at_piece] = cols_scr[:, :cut]
    late_ref[at_piece] = cols_scr[:, cut:]

    @pl.when(relative % 2 == 0)
    def _():
        even_ref[relative // 2] = cols_scr[...]

    @pl.when(relative % 2 == 1)
    def _():
        odd_ref[relative // 2] = cols_scr[...]


def whole(shape):
    return pl.BlockSpec(shape, lambda *a, n=len(shape): (0,) * n)


def call(kernel, place, inputs, in_specs, out_shapes, out_specs, scratch, steps, flops, alias=None):
    return pl.pallas_call(
        kernel,
        out_shape=out_shapes,
        grid_spec=pltpu.PrefetchScalarGridSpec(
            num_scalar_prefetch=1,
            grid=(steps,),
            in_specs=in_specs,
            out_specs=out_specs,
            scratch_shapes=scratch,
        ),
        input_output_aliases=alias or {},
        compiler_params=pltpu.CompilerParams(
            dimension_semantics=("arbitrary",), vmem_limit_bytes=16 << 20
        ),
        cost_estimate=pl.CostEstimate(flops=0, bytes_accessed=0, transcendentals=0),
    )(place, *inputs)


def in_hbm(x):
    return pltpu.with_memory_space_constraint(x, pltpu.HBM)


def flip(x, axis, mask):
    n = lax.axis_size(axis)
    return lax.ppermute(x, axis, [(i, i ^ mask) for i in range(n)])


def held(x, *others):
    return lax.optimization_barrier((x,) + others)[0]


def scan_send(total, mask):
    return flip(total.astype(bf16), "seq", mask) if mask < lax.axis_size("seq") else None


def scan_take(before, total, got, mask, reverse):
    got = got.astype(f32)
    upper = (lax.axis_index("seq") & mask) != 0
    return before + jnp.where(upper != reverse, got, 0.0), total.astype(f32) + got


def arrange_kernel(parts, *refs):
    pieces = refs[1 : 1 + parts]
    kept_ref, sent_ref = refs[1 + parts :]
    rows = pieces[0].shape[0]
    step = pl.program_id(0)
    half = pl.num_programs(0) // 2
    for target, on in ((kept_ref, step < half), (sent_ref, step >= half)):
        @pl.when(on)
        def _(target=target):
            for j in range(parts):
                target[j * rows : (j + 1) * rows, :] = pieces[j][...]


def arranged(pieces, masks):
    n, place = lax.axis_size("seq"), lax.axis_index("seq")
    order = [0]
    for mask in masks[::-1]:
        order = order + [j | mask for j in order]
    order = jnp.asarray(np.array(order, np.int32)) ^ place.astype(jnp.int32)
    parts = len(pieces)
    rows, depth = pieces[0].shape
    length, width, half = parts * rows, depth // n, depth // 2
    if width % 128:
        full = jnp.concatenate(pieces, axis=0).reshape(length, n, width)
        full = jnp.take(full, order, axis=1).reshape(length, depth)
        return full[:, :half], full[:, half:]
    out = pltpu.HBM((length, half), bf16)
    mid = n // 2
    return call(
        functools.partial(arrange_kernel, parts),
        order,
        list(pieces),
        [pl.BlockSpec((rows, width), lambda i, o: (0, o[i]))] * parts,
        [out, out],
        [
            pl.BlockSpec((length, width), lambda i, o: (0, jnp.minimum(i, mid - 1))),
            pl.BlockSpec((length, width), lambda i, o: (0, jnp.maximum(i - mid, 0))),
        ],
        [], n, 0,
    )


class Halve:
    def __init__(self, turn, left, right, scale, extra=None):
        n = lax.axis_size("seq")
        self.masks = [1 << b for b in range(n.bit_length() - 1)]
        self.turn = turn and n > 2
        if self.turn:
            self.masks = self.masks[1:] + self.masks[:1]
        self.left, self.right, self.scale, self.extra = left, right, scale, extra

    def product(self, side, *others):
        left = held(self.left, *others) if others else self.left
        n = lax.axis_size("seq")
        width = 2 * self.right[0].shape[1] // n
        if self.turn:
            half = self.right[0].shape[1] // 2
            pair = [
                (mm_tn(left, right[:, side * half : (side + 1) * half]) * self.scale).astype(bf16)
                for right in self.right
            ]
            out = jnp.concatenate(
                [p[:, i * width : (i + 1) * width] for i in range(n // 4) for p in pair], axis=1
            )
        else:
            out = (mm_tn(left, self.right[side]) * self.scale).astype(bf16)
        if self.extra is not None:
            tail = (self.extra[:4] * self.scale).astype(bf16).reshape(4, -1, width)
            tail = tail.transpose(1, 0, 2).reshape(-1, width)
            out = jnp.concatenate([out, jnp.tile(tail, (1, n // 2))], axis=0)
        return out

    def begin(self, *others):
        self.first = self.product(1, *others)
        self.got = flip(self.first, "seq", self.masks[0])
        self.at = 1

    def keep(self, *others):
        self.kept = [self.product(0, *others)]
        return self.kept[0]

    def step(self, *others):
        got = held(self.got, *others)
        self.kept.append(got)
        if self.at == len(self.masks):
            self.out = sum(t.astype(f32) for t in self.kept)
            return self.out
        half = got.shape[1] // 2
        send = sum(t[:, half:].astype(f32) for t in self.kept).astype(bf16)
        self.got = flip(send, "seq", self.masks[self.at])
        self.at += 1
        self.kept = [t[:, :half] for t in self.kept]
        return send


def masks_of(first):
    n = lax.axis_size("seq")
    masks = [1 << b for b in range(n.bit_length() - 1)]
    return masks[first:] + masks[:first]


def per_device(tokens_in, w_query, w_key, w_value, w_output, conv_taps, norm_gain, grad_out):
    nt, ns = lax.axis_size("tensor"), lax.axis_size("seq")
    rows, depth = tokens_in.shape
    length = rows * nt
    kw, vw = w_query.shape[1], w_value.shape[1]
    heads = vw // VD
    grad_scale = float(length * ns) ** -0.5
    place = lax.axis_index("tensor").reshape(1).astype(jnp.int32)
    e1q, e1k, e2, bias = feature_tables(heads)
    turned_q, turned_k, turned2 = e1q.T, e1k.T, e2.T
    turned_bias = jnp.pad(bias[:2].T, ((0, 0), (0, 126)))
    (
        e1q, e1k, e2, bias, turned_q, turned_k, turned2, turned_bias, conv_taps, norm_gain
    ) = (
        pltpu.with_memory_space_constraint(x, pltpu.HBM)
        for x in (
            e1q, e1k, e2, bias, turned_q, turned_k, turned2, turned_bias, conv_taps,
            norm_gain.reshape(1, -1),
        )
    )
    evens, odds = list(range(0, nt, 2)), list(range(1, nt, 2))

    far = {j: flip(tokens_in, "tensor", j) for j in evens[1:]}
    near = flip(tokens_in, "tensor", 1)
    near_cot = flip(grad_out, "tensor", 1)
    tail = held(tokens_in, near)[rows - 2 :]
    above = sum(
        lax.ppermute(
            tail, ("seq", "tensor"), [(s * nt + nt - 1, (s + 1) * nt + i) for s in range(ns - 1)]
        )
        for i in range(nt)
    )
    cw = vw + 2 * kw
    joined = [held(w, near) for w in (w_value, w_query, w_key)]
    weights = lax.optimization_barrier(jnp.concatenate(joined, axis=1))
    project = lambda piece: mm(piece, weights).astype(bf16)
    pull = lambda piece: mm_nt(piece, w_output).astype(bf16)
    halo = jnp.pad(mm(above, w_value).astype(bf16), ((6, 0), (0, 0)))
    tokens, cotangent = [tokens_in, near], [grad_out, near_cot]
    projected = [project(tokens_in), project(near)]
    pulled = [pull(grad_out), pull(near_cot)]
    for j in evens[1:]:
        piece = held(far[j], halo, *projected, *pulled)
        tokens += [piece, flip(piece, "tensor", 1)]
    projected += [project(piece) for piece in tokens[2:]]
    cot_from = held(grad_out, projected[2])
    far_cot = {j: flip(cot_from, "tensor", j) for j in evens[1:]}

    state_shape = (heads, STATE_ROWS, VD)
    at_chunk = lambda i, p: (i, 0)
    at_state = lambda i, p: (i, 0, 0, 0)
    on_chunk = lambda width: pl.BlockSpec((rows, width), at_chunk)
    state_spec = pl.BlockSpec((1,) + state_shape, at_state)
    square_spec = pl.BlockSpec((heads, rows, rows), lambda i, p: (0, i, 0))
    tables = [whole(e1q.shape), whole(e2.shape), whole(bias.shape)]
    turned_tables = [whole(turned_q.shape), whole(turned2.shape), whole(turned_bias.shape)]
    turned_spec = pl.BlockSpec((heads, LANES, rows), lambda i, p: (0, 0, i))
    shape = jax.ShapeDtypeStruct
    states_shape = shape((nt,) + state_shape, bf16)
    qk, values, mixed, states, total = call(
        functools.partial(conv_kernel, heads, list(range(heads)), nt),
        place,
        projected + [halo, conv_taps, turned_k, turned2, turned_bias],
        [whole((rows, cw))] * nt + [whole((8, vw)), whole((3, vw))] + turned_tables,
        [
            shape((length, 2 * kw), bf16),
            shape((length, vw), bf16),
            shape((length, vw), bf16),
            states_shape,
            shape(state_shape, bf16),
        ],
        [on_chunk(2 * kw), on_chunk(vw), on_chunk(vw), state_spec, whole(state_shape)],
        [pltpu.VMEM((rows, cw), bf16), pltpu.VMEM((8, vw), f32), pltpu.VMEM(state_shape, f32)],
        nt, 2 * length * vw * 256 * 3,
    )

    before = jnp.zeros(state_shape, f32)
    mask = 1
    got = scan_send(total, mask)
    pinned = lambda dims, kind: pltpu.HBM(dims, kind)
    local, phi, phi_t, weight, slope, prefix = call(
        functools.partial(pre_kernel, heads),
        place,
        [qk, mixed, states, e1q, e2, bias, turned_q, turned2, turned_bias],
        [on_chunk(2 * kw), on_chunk(vw), state_spec] + tables + turned_tables,
        [
            pinned((length, vw), bf16),
            pinned((length, heads * LANES), bf16),
            pinned((heads, LANES, length), bf16),
            pinned((heads, length, rows), bf16),
            pinned((heads, length, rows), bf16),
            states_shape,
        ],
        [
            on_chunk(vw), on_chunk(heads * LANES), turned_spec, square_spec, square_spec,
            state_spec,
        ],
        [pltpu.VMEM(state_shape, f32)],
        nt, 2 * length * vw * 256 * 5,
    )
    got = held(got, local)
    ordered = lambda pieces: [pieces[j] for j in evens + odds]
    while got is not None:
        before, total = scan_take(before, total, got, mask, False)
        mask *= 2
        got = scan_send(total, mask)
        if mask * 2 == ns:
            for j in evens[1:]:
                piece = held(far_cot[j], total)
                cotangent += [piece, flip(piece, "tensor", 1)]
            pulled += [pull(piece) for piece in cotangent[2:]]
            by_place = [pulled[j] for j in evens + odds]
            grad_attn = jnp.stack(by_place)
            ready = ordered(cotangent)
            ready[0] = held(ready[0], grad_attn)
            cot_for = arranged(ready, masks_of(0))
            got = held(got, *cot_for)
    carried = before.astype(bf16)

    half_shape = shape((nt // 2, rows, vw), bf16)
    slot = lambda j: (j >> 1) + (j & 1) * (nt // 2)
    attn_even, attn_odd, ds, gstates, gtotal, gain_sum, halo_out = call(
        functools.partial(mid_kernel, heads, nt),
        place,
        [
            local, phi, phi_t, carried, grad_attn, norm_gain, qk, weight, e1k, e2,
            bias,
        ],
        [
            on_chunk(vw),
            on_chunk(heads * LANES),
            turned_spec,
            whole(state_shape),
            pl.BlockSpec((1, rows, vw), lambda i, p: (slot(i ^ p[0]), 0, 0)),
            whole((1, vw)),
            whole((16, 2 * kw)),
            whole((heads, rows, 128)),
        ]
        + tables,
        [
            half_shape, half_shape, shape((length, vw), bf16), states_shape,
            shape(state_shape, bf16), shape((8, vw), f32), shape((8, vw + 2 * kw), f32),
        ],
        [
            whole(half_shape.shape), whole(half_shape.shape), on_chunk(vw), state_spec,
            whole(state_shape), whole((8, vw)), whole((8, vw + 2 * kw)),
        ],
        [pltpu.VMEM(state_shape, f32), pltpu.VMEM((rows, vw), bf16)],
        nt, 2 * length * vw * 256 * 2,
    )

    attn_all = jnp.concatenate([attn_even.reshape(-1, vw), attn_odd.reshape(-1, vw)], axis=0)
    ready = ordered(tokens)
    ready[0] = held(ready[0], gtotal)
    tokens_for = arranged(ready, masks_of(0))
    out_halve = Halve(False, attn_all, cot_for, grad_scale)
    after = jnp.zeros(state_shape, f32)
    got = scan_send(gtotal, 1)
    halo_in = lax.ppermute(halo_out, "seq", [(i + 1, i) for i in range(ns - 1)])
    out_odd = mm(attn_odd.reshape(-1, vw), w_output).astype(bf16)
    out_got = flip(out_odd, "tensor", 1)
    mask = 1
    while got is not None:
        cover = [out_odd, *tokens_for] if mask == 1 else [kept] if mask == 2 else [dv]
        after, gtotal = scan_take(after, gtotal, held(got, *cover), mask, True)
        mask *= 2
        got = scan_send(gtotal, mask)
        if mask == 2:
            out_flips = []
            out_rows = mm(attn_even.reshape(-1, vw), w_output) + held(out_got, gtotal).astype(f32)
            out_rows = out_rows.astype(bf16)
            for i in range(1, nt // 2):
                out_flips.append(flip(out_rows[i * rows : (i + 1) * rows], "tensor", 2 * i))
            out_halve.begin(out_rows)
            kept = out_halve.keep(out_halve.first)
        if mask == 4 or (mask == 2 and ns == 2):
            dqk, dv = call(
                functools.partial(post_kernel, heads),
                place,
                [
                    held(qk, gtotal), in_hbm(mixed), ds, in_hbm(weight), in_hbm(slope),
                    in_hbm(prefix), carried, e1q, e2, bias,
                ],
                [
                    on_chunk(2 * kw), on_chunk(vw), on_chunk(vw), square_spec, square_spec,
                    state_spec, whole(state_shape),
                ]
                + tables,
                [shape((length, 2 * kw), f32), shape((length, vw), bf16)],
                [on_chunk(2 * kw), on_chunk(vw)],
                [],
                nt, 2 * length * vw * 256 * 8,
            )
    gin = after.astype(bf16)
    dqk = held(dqk, out_halve.step(gin))

    last = lambda i, p: (nt - 1 - i, 0)
    from_last = lambda width: pl.BlockSpec((rows, width), last)
    cut = cw * 6 // 10 // 128 * 128
    early, late, cols_even, cols_odd, sums = call(
        functools.partial(finish_kernel, heads, cut, nt),
        place,
        [dqk, qk, values, mixed, dv, gstates, gin, conv_taps, halo_in, gain_sum, e1k, e2, bias],
        [
            from_last(2 * kw), from_last(2 * kw), from_last(vw), from_last(vw), from_last(vw),
            pl.BlockSpec((1,) + state_shape, lambda i, p: (nt - 1 - i, 0, 0, 0)),
            whole(state_shape), whole((3, vw)), whole((8, vw + 2 * kw)), whole((8, vw)),
        ]
        + tables,
        [
            shape((nt, rows, cut), bf16), shape((nt, rows, cw - cut), bf16),
            shape((nt // 2, rows, cw), bf16), shape((nt // 2, rows, cw), bf16),
            shape((8, vw), f32),
        ],
        [
            whole((nt, rows, cut)), whole((nt, rows, cw - cut)),
            whole((nt // 2, rows, cw)), whole((nt // 2, rows, cw)), whole((8, vw)),
        ],
        [
            pltpu.VMEM(state_shape, f32), pltpu.VMEM((8, vw), f32),
            pltpu.VMEM((rows, vw), f32), pltpu.VMEM((rows, cw), bf16),
        ],
        nt, 2 * length * vw * 256 * 6,
    )
    first = Halve(False, early.reshape(length, cut), tokens_for, grad_scale)
    out_flips = [held(got, early) for got in out_flips]
    steps = len(out_halve.masks)
    first = Halve(False, early.reshape(length, cut), tokens_for, grad_scale)
    first.begin(*out_flips)
    second = Halve(True, late.reshape(length, cw - cut), tokens_for, grad_scale, sums)
    done = out_halve.step(first.first) if steps > 2 else first.first
    second.begin(done)
    in_odd = mm_nt(held(cols_odd, second.first).reshape(-1, cw), weights).astype(bf16)
    in_got = held(flip(in_odd, "tensor", 1), in_odd)
    in_rows = mm_nt(cols_even.reshape(-1, cw), weights) + in_got.astype(f32)
    in_rows = in_rows.astype(bf16)
    in_flips = []
    for i in range(1, nt // 2):
        in_flips.append(flip(in_rows[i * rows : (i + 1) * rows], "tensor", 2 * i))
    done = first.keep(in_rows)
    done = first.step(done)
    done = second.keep(done)
    done = second.step(done)
    layer_out = held(out_rows, done)[:rows].astype(f32)
    for got in out_flips:
        layer_out += got.astype(f32)
    done = layer_out = layer_out.astype(bf16)
    for k in range(1, steps):
        if k < steps - 1 or steps == 2:
            done = out_halve.step(done)
        done = first.step(done) if k < steps - 1 else done
        done = second.step(done)
        if k == steps - 2 or steps == 2:
            grad_in = in_rows[:rows].astype(f32)
            for got in in_flips:
                grad_in += held(got, done).astype(f32)
            done = grad_in = grad_in.astype(bf16)
    first.step(done)
    while not hasattr(out_halve, "out"):
        out_halve.step(done)
    grad_wo = out_halve.out.astype(bf16)
    low, high = first.out.astype(bf16), second.out[: cw - cut].astype(bf16)
    sums = second.out[cw - cut :]
    sums = jnp.concatenate(jnp.split(sums, sums.shape[0] // 4, axis=0), axis=1)
    more = vw - cut
    grad_wv = jnp.concatenate([low.T, high[:more].T], axis=1)
    grad_wq = high[more : more + kw].T
    grad_wk = high[more + kw :].T
    return (layer_out, grad_in, grad_wq, grad_wk, grad_wv, grad_wo, sums[0:3], sums[3])


def solution(mesh):
    return jax.shard_map(
        per_device,
        mesh=mesh,
        in_specs=(
            P(("seq", "tensor"), None),
            P(None, "tensor"),
            P(None, "tensor"),
            P(None, "tensor"),
            P("tensor", None),
            P(None, "tensor"),
            P("tensor"),
            P(("seq", "tensor"), None),
        ),
        out_specs=(
            P(("seq", "tensor"), None),
            P(("seq", "tensor"), None),
            P("seq", "tensor"),
            P("seq", "tensor"),
            P("seq", "tensor"),
            P("tensor", "seq"),
            P(None, "tensor"),
            P("tensor"),
        ),
        check_vma=False,
    )
```

```python
import functools

import jax
import jax.numpy as jnp
import numpy as np
from jax import lax
from jax.experimental import pallas as pl
from jax.experimental.pallas import tpu as pltpu
from jax.sharding import PartitionSpec as P

VD = 128
FK = 16
FEATS = 153
STATE_ROWS = 160
LANES = 256
EPS = 1e-6

bf16 = jnp.bfloat16
f32 = jnp.float32
CONTRACT_COLS = (((1,), (1,)), ((), ()))
CONTRACT_ROWS = (((0,), (0,)), ((), ()))


def mm(a, b):
    return jnp.dot(a, b, preferred_element_type=f32)


def mm_nt(a, b):
    return lax.dot_general(a, b, CONTRACT_COLS, preferred_element_type=f32)


def mm_tn(a, b):
    return lax.dot_general(a, b, CONTRACT_ROWS, preferred_element_type=f32)


def feature_tables(heads):
    e1 = np.zeros((FK, LANES), np.float32)
    e2 = np.zeros((FK, LANES), np.float32)
    weight = np.zeros((LANES,), np.float32)
    bias = np.zeros((8, LANES), np.float32)
    bias[0, 0] = bias[1, 0] = weight[0] = 1.0
    for i in range(FK):
        e1[i, 1 + i] = 1.0
        bias[1, 1 + i] = 1.0
        weight[1 + i] = FK ** -0.5
    column = 1 + FK
    for i in range(FK):
        for j in range(i, FK):
            e1[i, column] = 1.0
            e2[j, column] = 1.0
            weight[column] = 1.0 / FK if i < j else 0.5 / FK
            column += 1
    def spread(table):
        out = np.zeros((heads, FK, heads, LANES), np.float32)
        for h in range(heads):
            out[h, :, h] = table
        return jnp.asarray(out.reshape(heads * FK, heads * LANES), bf16)
    return spread(e1), spread(e1 * weight), spread(e2), jnp.asarray(bias)


def features_t(rows, e1_ref, e2_ref, bias_ref, head):
    at = slice(head * LANES, (head + 1) * LANES)
    first = mm_nt(e1_ref[at, :], rows) + bias_ref[:, 0:1]
    second = mm_nt(e2_ref[at, :], rows) + bias_ref[:, 1:2]
    return (first * second).astype(bf16)


def features(rows, e1_ref, e2_ref, bias_ref, head):
    cols = slice(head * LANES, (head + 1) * LANES)
    first = mm(rows, e1_ref[:, cols]) + bias_ref[0:1, :]
    second = mm(rows, e2_ref[:, cols]) + bias_ref[1:2, :]
    return first, second


def features_pull(grad, first, second, e1_ref, e2_ref, head):
    cols = slice(head * LANES, (head + 1) * LANES)
    return mm_nt((grad * second).astype(bf16), e1_ref[:, cols]) + mm_nt(
        (grad * first).astype(bf16), e2_ref[:, cols]
    )


def head_only(rows, head, scale):
    lane = lax.broadcasted_iota(jnp.int32, rows.shape, 1)
    keep = (lane >= head * FK) & (lane < (head + 1) * FK)
    return jnp.where(keep, rows.astype(f32) * scale, 0.0).astype(bf16)


def full_state(state):
    return jnp.concatenate(
        [state.astype(bf16), jnp.zeros((LANES - STATE_ROWS, VD), bf16)], axis=0
    )


def conv_kernel(heads, group, parts, *refs):
    place_ref = refs[0]
    pieces = refs[1 : 1 + parts]
    halo_ref, taps_ref, e1_ref, e2_ref, bias_ref = refs[1 + parts : 6 + parts]
    qk_ref, v_ref, mixed_ref, state_ref, total_ref = refs[6 + parts : 11 + parts]
    piece_scr, prev_scr, total_scr = refs[11 + parts :]
    chunk = pl.program_id(0)
    relative = chunk ^ place_ref[0]
    for j in range(parts):
        @pl.when(relative == j)
        def _(j=j):
            piece_scr[...] = pieces[j][...]

    first_lane, last_lane = group[0] * VD, (group[-1] + 1) * VD

    @pl.when(chunk == 0)
    def _():
        prev_scr[...] = halo_ref[:, first_lane:last_lane].astype(f32)
        total_scr[...] = jnp.zeros_like(total_scr)

    vw = heads * VD
    kw = heads * FK
    values = piece_scr[:, first_lane:last_lane]
    qk = piece_scr[:, vw : vw + 2 * kw]
    k = qk[:, kw:]
    qk_ref[...] = qk
    v_ref[...] = values
    wide = values.astype(f32)
    rows = wide.shape[0]
    at = lax.broadcasted_iota(jnp.int32, wide.shape, 0)
    before1 = prev_scr[7:8, :]
    before2 = prev_scr[6:7, :]
    lag1 = jnp.where(at == 0, before1, pltpu.roll(wide, 1, 0))
    lag2 = jnp.where(at == 0, before2, jnp.where(at == 1, before1, pltpu.roll(wide, 2, 0)))
    prev_scr[...] = wide[rows - 8 :, :]
    taps = taps_ref[:, first_lane:last_lane]
    mixed = (taps[0:1, :] * wide + taps[1:2, :] * lag1 + taps[2:3, :] * lag2).astype(bf16)
    mixed_ref[...] = mixed
    for i, h in enumerate(group):
        phi_t = features_t(k, e1_ref, e2_ref, bias_ref, h)
        state = mm(phi_t, mixed[:, i * VD : (i + 1) * VD])[:STATE_ROWS]
        state_ref[0, i] = state.astype(bf16)
        total_scr[i] += state

    @pl.when(chunk == pl.num_programs(0) - 1)
    def _():
        total_ref[...] = total_scr[...].astype(bf16)


def pre_kernel(heads, *refs):
    (
        _, qk_ref, mixed_ref, state_ref, e1_ref, e2_ref, bias_ref, e1t_ref, e2t_ref, biast_ref,
        local_ref, phi_ref, turned_ref, weight_ref, slope_ref, prefix_ref,
        run_scr,
    ) = refs

    @pl.when(pl.program_id(0) == 0)
    def _():
        run_scr[...] = jnp.zeros_like(run_scr)

    kw = heads * FK
    q = qk_ref[:, :kw]
    k = qk_ref[:, kw:]
    rows = q.shape[0]
    row = lax.broadcasted_iota(jnp.int32, (rows, rows), 0)
    col = lax.broadcasted_iota(jnp.int32, (rows, rows), 1)
    causal = row >= col
    for h in range(heads):
        lanes = slice(h * VD, (h + 1) * VD)
        first, second = features(q, e1_ref, e2_ref, bias_ref, h)
        phi = (first * second).astype(bf16)
        phi_ref[:, h * LANES : (h + 1) * LANES] = phi
        turned_ref[h] = features_t(q, e1t_ref, e2t_ref, biast_ref, h)
        u = mm_nt(q, head_only(k, h, FK ** -0.5))
        slope = 1.0 + u
        weight = jnp.where(causal, slope + 0.5 * u * u, 0.0).astype(bf16)
        weight_ref[h] = weight
        slope_ref[h] = jnp.where(causal, slope, 0.0).astype(bf16)
        prefix = run_scr[h].astype(bf16)
        prefix_ref[0, h] = prefix
        local = mm(weight, mixed_ref[:, lanes]) + mm(phi, full_state(prefix))
        local_ref[:, lanes] = local.astype(bf16)
        run_scr[h] += state_ref[0, h].astype(f32)


def mid_kernel(heads, parts, *refs):
    (
        place_ref, local_ref, phi_ref, turned_ref, carried_ref, ga_ref, gain_ref,
        qk_ref, weight_ref, e1k_ref, e2_ref, bias_ref,
        even_ref, odd_ref, ds_ref, gstate_ref, gtotal_ref, gain_sum_ref, halo_ref,
        gtotal_scr, attn_scr,
    ) = refs
    chunk = pl.program_id(0)
    relative = chunk ^ place_ref[0]

    @pl.when(chunk == 0)
    def _():
        gtotal_scr[...] = jnp.zeros_like(gtotal_scr)
        gain_sum_ref[...] = jnp.zeros_like(gain_sum_ref)

    for h in range(heads):
        lanes = slice(h * VD, (h + 1) * VD)
        phi = phi_ref[:, h * LANES : (h + 1) * LANES]
        summed = local_ref[:, lanes].astype(f32) + mm(phi, full_state(carried_ref[h]))
        scale = lax.rsqrt(jnp.mean(summed * summed, axis=-1, keepdims=True) + EPS)
        unit = summed * scale
        gain = gain_ref[0:1, lanes]
        attn_scr[:, lanes] = (unit * gain).astype(bf16)
        ga = ga_ref[0, :, lanes].astype(f32)
        gu = ga * unit
        gain_sum_ref[0:1, lanes] += jnp.sum(gu, axis=0, keepdims=True)
        ds = scale * (ga * gain - unit * jnp.mean(gu * gain, axis=-1, keepdims=True))
        ds = ds.astype(bf16)
        ds_ref[:, lanes] = ds
        gstate = mm(turned_ref[h], ds)[:STATE_ROWS]
        gstate_ref[0, h] = gstate.astype(bf16)
        gtotal_scr[h] += gstate

    @pl.when(chunk == 0)
    def _():
        kw = heads * FK
        vw = heads * VD
        qk = qk_ref[...]
        for h in range(heads):
            lanes = slice(h * VD, (h + 1) * VD)
            kfirst, ksecond = features(qk[:, kw:], e1k_ref, e2_ref, bias_ref, h)
            kphi = (kfirst * ksecond).astype(bf16)
            own = mm(kphi, full_state(gstate_ref[0, h]))
            top = mm_tn(weight_ref[h], ds_ref[:, lanes])
            halo_ref[:, lanes] = top[0:8] - own[0:8]
        halo_ref[:, vw:] = qk[0:8, :].astype(f32)

    @pl.when(relative % 2 == 0)
    def _():
        even_ref[relative // 2] = attn_scr[...]

    @pl.when(relative % 2 == 1)
    def _():
        odd_ref[relative // 2] = attn_scr[...]

    @pl.when(chunk == pl.num_programs(0) - 1)
    def _():
        gtotal_ref[...] = gtotal_scr[...].astype(bf16)


def post_kernel(heads, *refs):
    (
        _, qk_ref, mixed_ref, ds_ref, weight_ref, slope_ref, prefix_ref, carried_ref,
        e1q_ref, e2_ref, bias_ref,
        dqk_ref, dv_ref,
    ) = refs
    kw = heads * FK
    qk = qk_ref[...]
    q = qk[:, :kw]
    k = qk[:, kw:]
    dq = jnp.zeros(q.shape, f32)
    dk = jnp.zeros(q.shape, f32)
    for h in range(heads):
        lanes = slice(h * VD, (h + 1) * VD)
        ds = ds_ref[:, lanes]
        dw = mm_nt(ds, mixed_ref[:, lanes]).astype(bf16).astype(f32)
        du = (dw * slope_ref[h].astype(f32)).astype(bf16)
        dq += mm(du, head_only(k, h, FK ** -0.5))
        dk += mm_tn(du, head_only(q, h, FK ** -0.5))
        dv_ref[:, lanes] = mm_tn(weight_ref[h], ds).astype(bf16)
        state = full_state(prefix_ref[0, h].astype(f32) + carried_ref[h].astype(f32))
        first, second = features(q, e1q_ref, e2_ref, bias_ref, h)
        dq += features_pull(mm_nt(ds, state), first, second, e1q_ref, e2_ref, h)
    dqk_ref[:, :kw] = dq
    dqk_ref[:, kw:] = dk


def finish_kernel(heads, cut, parts, *refs):
    (
        place_ref, dqk_ref, qk_ref, v_ref, mixed_ref, dv_ref, gstate_ref, gin_ref,
        taps_ref, halo_ref, gain_ref, e1_ref, e2_ref, bias_ref,
        early_ref, late_ref, even_ref, odd_ref, sums_ref,
        run_scr, next_scr, mixed_scr, cols_scr,
    ) = refs
    step = pl.program_id(0)
    chunk = pl.num_programs(0) - 1 - step
    relative = chunk ^ place_ref[0]
    kw = heads * FK
    vw = heads * VD

    @pl.when(step == 0)
    def _():
        run_scr[...] = gin_ref[...].astype(f32)
        sums_ref[...] = jnp.zeros_like(sums_ref)
        sums_ref[3:4, :] = gain_ref[0:1, :]
        hk = jnp.concatenate([halo_ref[:, vw + kw :]] * 2, axis=0).astype(bf16)
        for h in range(heads):
            lanes = slice(h * VD, (h + 1) * VD)
            first, second = features(hk, e1_ref, e2_ref, bias_ref, h)
            phi = (first * second).astype(bf16)
            next_scr[:, lanes] = halo_ref[:, lanes] + mm(phi, full_state(gin_ref[h]))[0:8]

    k = qk_ref[:, kw:]
    dk = dqk_ref[:, kw:]
    for h in range(heads):
        lanes = slice(h * VD, (h + 1) * VD)
        first, second = features(k, e1_ref, e2_ref, bias_ref, h)
        phi = (first * second).astype(bf16)
        state = full_state(run_scr[h])
        mixed_scr[:, lanes] = dv_ref[:, lanes].astype(f32) + mm(phi, state)
        dphi = mm_nt(mixed_ref[:, lanes], state)
        dk += features_pull(dphi, first, second, e1_ref, e2_ref, h)
        run_scr[h] += gstate_ref[0, h].astype(f32)
    gm = mixed_scr[...]
    rows = gm.shape[0]
    at = lax.broadcasted_iota(jnp.int32, gm.shape, 0)
    after0 = next_scr[0:1, :]
    after1 = next_scr[1:2, :]
    lead1 = jnp.where(at == rows - 1, after0, pltpu.roll(gm, rows - 1, 0))
    lead2 = jnp.where(
        at == rows - 1, after1, jnp.where(at == rows - 2, after0, pltpu.roll(gm, rows - 2, 0))
    )
    next_scr[...] = gm[0:8, :]
    gv = taps_ref[0:1, :] * gm + taps_ref[1:2, :] * lead1 + taps_ref[2:3, :] * lead2
    values = v_ref[...].astype(f32)
    sums_ref[0:1, :] += jnp.sum(gm * values, axis=0, keepdims=True)
    sums_ref[1:2, :] += jnp.sum(lead1 * values, axis=0, keepdims=True)
    sums_ref[2:3, :] += jnp.sum(lead2 * values, axis=0, keepdims=True)
    cols_scr[:, :vw] = gv.astype(bf16)
    cols_scr[:, vw : vw + kw] = dqk_ref[:, :kw].astype(bf16)
    cols_scr[:, vw + kw :] = dk.astype(bf16)
    at_piece = relative // 2 + (relative % 2) * (parts // 2)
    early_ref[at_piece] = cols_scr[:, :cut]
    late_ref[at_piece] = cols_scr[:, cut:]

    @pl.when(relative % 2 == 0)
    def _():
        even_ref[relative // 2] = cols_scr[...]

    @pl.when(relative % 2 == 1)
    def _():
        odd_ref[relative // 2] = cols_scr[...]


def whole(shape):
    return pl.BlockSpec(shape, lambda *a, n=len(shape): (0,) * n)


def call(kernel, place, inputs, in_specs, out_shapes, out_specs, scratch, steps, flops, alias=None):
    return pl.pallas_call(
        kernel,
        out_shape=out_shapes,
        grid_spec=pltpu.PrefetchScalarGridSpec(
            num_scalar_prefetch=1,
            grid=(steps,),
            in_specs=in_specs,
            out_specs=out_specs,
            scratch_shapes=scratch,
        ),
        input_output_aliases=alias or {},
        compiler_params=pltpu.CompilerParams(
            dimension_semantics=("arbitrary",), vmem_limit_bytes=16 << 20
        ),
        cost_estimate=pl.CostEstimate(flops=0, bytes_accessed=0, transcendentals=0),
    )(place, *inputs)


def in_hbm(x):
    return pltpu.with_memory_space_constraint(x, pltpu.HBM)


def flip(x, axis, mask):
    n = lax.axis_size(axis)
    return lax.ppermute(x, axis, [(i, i ^ mask) for i in range(n)])


def held(x, *others):
    return lax.optimization_barrier((x,) + others)[0]


def scan_send(total, mask):
    return flip(total.astype(bf16), "seq", mask) if mask < lax.axis_size("seq") else None


def scan_take(before, total, got, mask, reverse):
    got = got.astype(f32)
    upper = (lax.axis_index("seq") & mask) != 0
    return before + jnp.where(upper != reverse, got, 0.0), total.astype(f32) + got


def arrange_kernel(parts, *refs):
    pieces = refs[1 : 1 + parts]
    kept_ref, sent_ref = refs[1 + parts :]
    rows = pieces[0].shape[0]
    step = pl.program_id(0)
    half = pl.num_programs(0) // 2
    for target, on in ((kept_ref, step < half), (sent_ref, step >= half)):
        @pl.when(on)
        def _(target=target):
            for j in range(parts):
                target[j * rows : (j + 1) * rows, :] = pieces[j][...]


def arranged(pieces, masks):
    n, place = lax.axis_size("seq"), lax.axis_index("seq")
    order = [0]
    for mask in masks[::-1]:
        order = order + [j | mask for j in order]
    order = jnp.asarray(np.array(order, np.int32)) ^ place.astype(jnp.int32)
    parts = len(pieces)
    rows, depth = pieces[0].shape
    length, width, half = parts * rows, depth // n, depth // 2
    if width % 128:
        full = jnp.concatenate(pieces, axis=0).reshape(length, n, width)
        full = jnp.take(full, order, axis=1).reshape(length, depth)
        return full[:, :half], full[:, half:]
    out = pltpu.HBM((length, half), bf16)
    mid = n // 2
    return call(
        functools.partial(arrange_kernel, parts),
        order,
        list(pieces),
        [pl.BlockSpec((rows, width), lambda i, o: (0, o[i]))] * parts,
        [out, out],
        [
            pl.BlockSpec((length, width), lambda i, o: (0, jnp.minimum(i, mid - 1))),
            pl.BlockSpec((length, width), lambda i, o: (0, jnp.maximum(i - mid, 0))),
        ],
        [], n, 0,
    )


class Halve:
    def __init__(self, turn, left, right, scale, extra=None):
        n = lax.axis_size("seq")
        self.masks = [1 << b for b in range(n.bit_length() - 1)]
        self.turn = turn and n > 2
        if self.turn:
            self.masks = self.masks[1:] + self.masks[:1]
        self.left, self.right, self.scale, self.extra = left, right, scale, extra

    def product(self, side, *others):
        left = held(self.left, *others) if others else self.left
        n = lax.axis_size("seq")
        width = 2 * self.right[0].shape[1] // n
        if self.turn:
            half = self.right[0].shape[1] // 2
            pair = [
                (mm_tn(left, right[:, side * half : (side + 1) * half]) * self.scale).astype(bf16)
                for right in self.right
            ]
            out = jnp.concatenate(
                [p[:, i * width : (i + 1) * width] for i in range(n // 4) for p in pair], axis=1
            )
        else:
            out = (mm_tn(left, self.right[side]) * self.scale).astype(bf16)
        if self.extra is not None:
            tail = (self.extra[:4] * self.scale).astype(bf16).reshape(4, -1, width)
            tail = tail.transpose(1, 0, 2).reshape(-1, width)
            out = jnp.concatenate([out, jnp.tile(tail, (1, n // 2))], axis=0)
        return out

    def begin(self, *others):
        self.first = self.product(1, *others)
        self.got = flip(self.first, "seq", self.masks[0])
        self.at = 1

    def keep(self, *others):
        self.kept = [self.product(0, *others)]
        return self.kept[0]

    def step(self, *others):
        got = held(self.got, *others)
        self.kept.append(got)
        if self.at == len(self.masks):
            self.out = sum(t.astype(f32) for t in self.kept)
            return self.out
        half = got.shape[1] // 2
        send = sum(t[:, half:].astype(f32) for t in self.kept).astype(bf16)
        self.got = flip(send, "seq", self.masks[self.at])
        self.at += 1
        self.kept = [t[:, :half] for t in self.kept]
        return send


def product_kernel(_, left_ref, right_ref, *refs):
    total = mm_nt(left_ref[...], right_ref[...])
    if len(refs) > 1:
        total += refs[0][...].astype(f32)
    refs[-1][...] = total.astype(bf16)


def product_nt(left, right, place, *more):
    height, width = left.shape[0], right.shape[0]
    tile = min(width, 1024)
    columns = pl.BlockSpec((height, tile), lambda i, p: (0, i))
    return call(
        product_kernel,
        place,
        [left, right, *more],
        [whole(left.shape), pl.BlockSpec((tile, right.shape[1]), lambda i, p: (i, 0))]
        + [columns] * len(more),
        [jax.ShapeDtypeStruct((height, width), bf16)],
        [columns],
        [], width // tile, 0,
    )[0]


def masks_of(first):
    n = lax.axis_size("seq")
    masks = [1 << b for b in range(n.bit_length() - 1)]
    return masks[first:] + masks[:first]


def per_device(tokens_in, w_query, w_key, w_value, w_output, conv_taps, norm_gain, grad_out):
    nt, ns = lax.axis_size("tensor"), lax.axis_size("seq")
    rows, depth = tokens_in.shape
    length = rows * nt
    kw, vw = w_query.shape[1], w_value.shape[1]
    heads = vw // VD
    grad_scale = float(length * ns) ** -0.5
    place = lax.axis_index("tensor").reshape(1).astype(jnp.int32)
    e1q, e1k, e2, bias = feature_tables(heads)
    turned_q, turned_k, turned2 = e1q.T, e1k.T, e2.T
    turned_bias = jnp.pad(bias[:2].T, ((0, 0), (0, 126)))
    (
        e1q, e1k, e2, bias, turned_q, turned_k, turned2, turned_bias, conv_taps, norm_gain
    ) = (
        pltpu.with_memory_space_constraint(x, pltpu.HBM)
        for x in (
            e1q, e1k, e2, bias, turned_q, turned_k, turned2, turned_bias, conv_taps,
            norm_gain.reshape(1, -1),
        )
    )
    evens, odds = list(range(0, nt, 2)), list(range(1, nt, 2))

    far = {j: flip(tokens_in, "tensor", j) for j in evens[1:]}
    near = flip(tokens_in, "tensor", 1)
    near_cot = flip(grad_out, "tensor", 1)
    tail = held(tokens_in, near)[rows - 2 :]
    above = sum(
        lax.ppermute(
            tail, ("seq", "tensor"), [(s * nt + nt - 1, (s + 1) * nt + i) for s in range(ns - 1)]
        )
        for i in range(nt)
    )
    cw = vw + 2 * kw
    joined = [held(w, near) for w in (w_value, w_query, w_key)]
    weights = lax.optimization_barrier(jnp.concatenate(joined, axis=1))
    project = lambda piece: mm(piece, weights).astype(bf16)
    pull = lambda piece: mm_nt(piece, w_output).astype(bf16)
    halo = jnp.pad(mm(above, w_value).astype(bf16), ((6, 0), (0, 0)))
    tokens, cotangent = [tokens_in, near], [grad_out, near_cot]
    projected = [project(tokens_in), project(near)]
    pulled = [pull(grad_out), pull(near_cot)]
    for j in evens[1:]:
        piece = held(far[j], halo, *projected, *pulled)
        tokens += [piece, flip(piece, "tensor", 1)]
    projected += [project(piece) for piece in tokens[2:]]
    cot_from = held(grad_out, projected[2])
    far_cot = {j: flip(cot_from, "tensor", j) for j in evens[1:]}

    state_shape = (heads, STATE_ROWS, VD)
    at_chunk = lambda i, p: (i, 0)
    at_state = lambda i, p: (i, 0, 0, 0)
    on_chunk = lambda width: pl.BlockSpec((rows, width), at_chunk)
    state_spec = pl.BlockSpec((1,) + state_shape, at_state)
    square_spec = pl.BlockSpec((heads, rows, rows), lambda i, p: (0, i, 0))
    tables = [whole(e1q.shape), whole(e2.shape), whole(bias.shape)]
    turned_tables = [whole(turned_q.shape), whole(turned2.shape), whole(turned_bias.shape)]
    turned_spec = pl.BlockSpec((heads, LANES, rows), lambda i, p: (0, 0, i))
    shape = jax.ShapeDtypeStruct
    states_shape = shape((nt,) + state_shape, bf16)
    qk, values, mixed, states, total = call(
        functools.partial(conv_kernel, heads, list(range(heads)), nt),
        place,
        projected + [halo, conv_taps, turned_k, turned2, turned_bias],
        [whole((rows, cw))] * nt + [whole((8, vw)), whole((3, vw))] + turned_tables,
        [
            shape((length, 2 * kw), bf16),
            shape((length, vw), bf16),
            shape((length, vw), bf16),
            states_shape,
            shape(state_shape, bf16),
        ],
        [on_chunk(2 * kw), on_chunk(vw), on_chunk(vw), state_spec, whole(state_shape)],
        [pltpu.VMEM((rows, cw), bf16), pltpu.VMEM((8, vw), f32), pltpu.VMEM(state_shape, f32)],
        nt, 2 * length * vw * 256 * 3,
    )

    before = jnp.zeros(state_shape, f32)
    mask = 1
    got = scan_send(total, mask)
    pinned = lambda dims, kind: pltpu.HBM(dims, kind)
    local, phi, phi_t, weight, slope, prefix = call(
        functools.partial(pre_kernel, heads),
        place,
        [qk, mixed, states, e1q, e2, bias, turned_q, turned2, turned_bias],
        [on_chunk(2 * kw), on_chunk(vw), state_spec] + tables + turned_tables,
        [
            pinned((length, vw), bf16),
            pinned((length, heads * LANES), bf16),
            pinned((heads, LANES, length), bf16),
            pinned((heads, length, rows), bf16),
            pinned((heads, length, rows), bf16),
            states_shape,
        ],
        [
            on_chunk(vw), on_chunk(heads * LANES), turned_spec, square_spec, square_spec,
            state_spec,
        ],
        [pltpu.VMEM(state_shape, f32)],
        nt, 2 * length * vw * 256 * 5,
    )
    got = held(got, local)
    ordered = lambda pieces: [pieces[j] for j in evens + odds]
    while got is not None:
        before, total = scan_take(before, total, got, mask, False)
        mask *= 2
        got = scan_send(total, mask)
        if mask * 2 == ns:
            for j in evens[1:]:
                piece = held(far_cot[j], total)
                cotangent += [piece, flip(piece, "tensor", 1)]
            pulled += [pull(piece) for piece in cotangent[2:]]
            by_place = [pulled[j] for j in evens + odds]
            grad_attn = jnp.stack(by_place)
            ready = ordered(cotangent)
            ready[0] = held(ready[0], grad_attn)
            cot_for = arranged(ready, masks_of(0))
            got = held(got, *cot_for)
    carried = before.astype(bf16)

    half_shape = shape((nt // 2, rows, vw), bf16)
    slot = lambda j: (j >> 1) + (j & 1) * (nt // 2)
    attn_even, attn_odd, ds, gstates, gtotal, gain_sum, halo_out = call(
        functools.partial(mid_kernel, heads, nt),
        place,
        [
            local, phi, phi_t, carried, grad_attn, norm_gain, qk, weight, e1k, e2,
            bias,
        ],
        [
            on_chunk(vw),
            on_chunk(heads * LANES),
            turned_spec,
            whole(state_shape),
            pl.BlockSpec((1, rows, vw), lambda i, p: (slot(i ^ p[0]), 0, 0)),
            whole((1, vw)),
            whole((16, 2 * kw)),
            whole((heads, rows, 128)),
        ]
        + tables,
        [
            half_shape, half_shape, shape((length, vw), bf16), states_shape,
            shape(state_shape, bf16), shape((8, vw), f32), shape((8, vw + 2 * kw), f32),
        ],
        [
            whole(half_shape.shape), whole(half_shape.shape), on_chunk(vw), state_spec,
            whole(state_shape), whole((8, vw)), whole((8, vw + 2 * kw)),
        ],
        [pltpu.VMEM(state_shape, f32), pltpu.VMEM((rows, vw), bf16)],
        nt, 2 * length * vw * 256 * 2,
    )

    attn_all = jnp.concatenate([attn_even.reshape(-1, vw), attn_odd.reshape(-1, vw)], axis=0)
    ready = ordered(tokens)
    ready[0] = held(ready[0], gtotal)
    tokens_for = arranged(ready, masks_of(0))
    out_halve = Halve(False, attn_all, cot_for, grad_scale)
    after = jnp.zeros(state_shape, f32)
    got = scan_send(gtotal, 1)
    halo_in = lax.ppermute(halo_out, "seq", [(i + 1, i) for i in range(ns - 1)])
    out_odd = mm(attn_odd.reshape(-1, vw), w_output).astype(bf16)
    out_got = flip(out_odd, "tensor", 1)
    mask = 1
    while got is not None:
        cover = [out_odd, *tokens_for] if mask == 1 else [kept] if mask == 2 else [dv]
        after, gtotal = scan_take(after, gtotal, held(got, *cover), mask, True)
        mask *= 2
        got = scan_send(gtotal, mask)
        if mask == 2:
            out_flips = []
            out_rows = mm(attn_even.reshape(-1, vw), w_output) + held(out_got, gtotal).astype(f32)
            out_rows = out_rows.astype(bf16)
            for i in range(1, nt // 2):
                out_flips.append(flip(out_rows[i * rows : (i + 1) * rows], "tensor", 2 * i))
            out_halve.begin(out_rows)
            kept = out_halve.keep(out_halve.first)
        if mask == 4 or (mask == 2 and ns == 2):
            dqk, dv = call(
                functools.partial(post_kernel, heads),
                place,
                [
                    held(qk, gtotal), in_hbm(mixed), ds, in_hbm(weight), in_hbm(slope),
                    in_hbm(prefix), carried, e1q, e2, bias,
                ],
                [
                    on_chunk(2 * kw), on_chunk(vw), on_chunk(vw), square_spec, square_spec,
                    state_spec, whole(state_shape),
                ]
                + tables,
                [shape((length, 2 * kw), f32), shape((length, vw), bf16)],
                [on_chunk(2 * kw), on_chunk(vw)],
                [],
                nt, 2 * length * vw * 256 * 8,
            )
    gin = after.astype(bf16)
    dqk = held(dqk, out_halve.step(gin))

    last = lambda i, p: (nt - 1 - i, 0)
    from_last = lambda width: pl.BlockSpec((rows, width), last)
    cut = cw * 6 // 10 // 128 * 128
    early, late, cols_even, cols_odd, sums = call(
        functools.partial(finish_kernel, heads, cut, nt),
        place,
        [dqk, qk, values, mixed, dv, gstates, gin, conv_taps, halo_in, gain_sum, e1k, e2, bias],
        [
            from_last(2 * kw), from_last(2 * kw), from_last(vw), from_last(vw), from_last(vw),
            pl.BlockSpec((1,) + state_shape, lambda i, p: (nt - 1 - i, 0, 0, 0)),
            whole(state_shape), whole((3, vw)), whole((8, vw + 2 * kw)), whole((8, vw)),
        ]
        + tables,
        [
            shape((nt, rows, cut), bf16), shape((nt, rows, cw - cut), bf16),
            shape((nt // 2, rows, cw), bf16), shape((nt // 2, rows, cw), bf16),
            shape((8, vw), f32),
        ],
        [
            whole((nt, rows, cut)), whole((nt, rows, cw - cut)),
            whole((nt // 2, rows, cw)), whole((nt // 2, rows, cw)), whole((8, vw)),
        ],
        [
            pltpu.VMEM(state_shape, f32), pltpu.VMEM((8, vw), f32),
            pltpu.VMEM((rows, vw), f32), pltpu.VMEM((rows, cw), bf16),
        ],
        nt, 2 * length * vw * 256 * 6,
    )
    first = Halve(False, early.reshape(length, cut), tokens_for, grad_scale)
    out_flips = [held(got, early) for got in out_flips]
    steps = len(out_halve.masks)
    first = Halve(False, early.reshape(length, cut), tokens_for, grad_scale)
    first.begin(*out_flips)
    second = Halve(True, late.reshape(length, cw - cut), tokens_for, grad_scale, sums)
    done = out_halve.step(first.first) if steps > 2 else first.first
    second.begin(done)
    in_odd = product_nt(held(cols_odd, second.first).reshape(-1, cw), weights, place)
    in_got = held(flip(in_odd, "tensor", 1), in_odd)
    in_rows = mm_nt(cols_even.reshape(-1, cw), weights) + in_got.astype(f32)
    in_rows = in_rows.astype(bf16)
    in_flips = []
    for i in range(1, nt // 2):
        in_flips.append(flip(in_rows[i * rows : (i + 1) * rows], "tensor", 2 * i))
    done = first.keep(in_rows)
    done = first.step(done)
    done = second.keep(done)
    done = second.step(done)
    layer_out = held(out_rows, done)[:rows].astype(f32)
    for got in out_flips:
        layer_out += got.astype(f32)
    done = layer_out = layer_out.astype(bf16)
    for k in range(1, steps):
        done = first.step(done) if k < steps - 1 else done
        done = second.step(done)
        if k < steps - 1 or steps == 2:
            done = out_halve.step(done)
        if k == steps - 2 or steps == 2:
            grad_in = in_rows[:rows].astype(f32)
            for got in in_flips:
                grad_in += held(got, done).astype(f32)
            done = grad_in = grad_in.astype(bf16)
    first.step(done)
    while not hasattr(out_halve, "out"):
        out_halve.step(done)
    grad_wo = out_halve.out.astype(bf16)
    low, high = first.out.astype(bf16), second.out[: cw - cut].astype(bf16)
    sums = second.out[cw - cut :]
    sums = jnp.concatenate(jnp.split(sums, sums.shape[0] // 4, axis=0), axis=1)
    more = vw - cut
    grad_wv = jnp.concatenate([low.T, high[:more].T], axis=1)
    grad_wq = high[more : more + kw].T
    grad_wk = high[more + kw :].T
    return (layer_out, grad_in, grad_wq, grad_wk, grad_wv, grad_wo, sums[0:3], sums[3])


def solution(mesh):
    return jax.shard_map(
        per_device,
        mesh=mesh,
        in_specs=(
            P(("seq", "tensor"), None),
            P(None, "tensor"),
            P(None, "tensor"),
            P(None, "tensor"),
            P("tensor", None),
            P(None, "tensor"),
            P("tensor"),
            P(("seq", "tensor"), None),
        ),
        out_specs=(
            P(("seq", "tensor"), None),
            P(("seq", "tensor"), None),
            P("seq", "tensor"),
            P("seq", "tensor"),
            P("seq", "tensor"),
            P("tensor", "seq"),
            P(None, "tensor"),
            P("tensor"),
        ),
        check_vma=False,
    )
```

```python
import functools

import jax
import jax.numpy as jnp
import numpy as np
from jax import lax
from jax.experimental import pallas as pl
from jax.experimental.pallas import tpu as pltpu
from jax.sharding import PartitionSpec as P

VD = 128
FK = 16
FEATS = 153
STATE_ROWS = 160
LANES = 256
EPS = 1e-6

bf16 = jnp.bfloat16
f32 = jnp.float32
CONTRACT_COLS = (((1,), (1,)), ((), ()))
CONTRACT_ROWS = (((0,), (0,)), ((), ()))


def mm(a, b):
    return jnp.dot(a, b, preferred_element_type=f32)


def mm_nt(a, b):
    return lax.dot_general(a, b, CONTRACT_COLS, preferred_element_type=f32)


def mm_tn(a, b):
    return lax.dot_general(a, b, CONTRACT_ROWS, preferred_element_type=f32)


def feature_tables(heads):
    e1 = np.zeros((FK, LANES), np.float32)
    e2 = np.zeros((FK, LANES), np.float32)
    weight = np.zeros((LANES,), np.float32)
    bias = np.zeros((8, LANES), np.float32)
    bias[0, 0] = bias[1, 0] = weight[0] = 1.0
    for i in range(FK):
        e1[i, 1 + i] = 1.0
        bias[1, 1 + i] = 1.0
        weight[1 + i] = FK ** -0.5
    column = 1 + FK
    for i in range(FK):
        for j in range(i, FK):
            e1[i, column] = 1.0
            e2[j, column] = 1.0
            weight[column] = 1.0 / FK if i < j else 0.5 / FK
            column += 1
    def spread(table):
        out = np.zeros((heads, FK, heads, LANES), np.float32)
        for h in range(heads):
            out[h, :, h] = table
        return jnp.asarray(out.reshape(heads * FK, heads * LANES), bf16)
    return spread(e1), spread(e1 * weight), spread(e2), jnp.asarray(bias)


def features_t(rows, e1_ref, e2_ref, bias_ref, head):
    at = slice(head * LANES, (head + 1) * LANES)
    first = mm_nt(e1_ref[at, :], rows) + bias_ref[:, 0:1]
    second = mm_nt(e2_ref[at, :], rows) + bias_ref[:, 1:2]
    return (first * second).astype(bf16)


def features(rows, e1_ref, e2_ref, bias_ref, head):
    cols = slice(head * LANES, (head + 1) * LANES)
    first = mm(rows, e1_ref[:, cols]) + bias_ref[0:1, :]
    second = mm(rows, e2_ref[:, cols]) + bias_ref[1:2, :]
    return first, second


def features_pull(grad, first, second, e1_ref, e2_ref, head):
    cols = slice(head * LANES, (head + 1) * LANES)
    return mm_nt((grad * second).astype(bf16), e1_ref[:, cols]) + mm_nt(
        (grad * first).astype(bf16), e2_ref[:, cols]
    )


def head_only(rows, head, scale):
    lane = lax.broadcasted_iota(jnp.int32, rows.shape, 1)
    keep = (lane >= head * FK) & (lane < (head + 1) * FK)
    return jnp.where(keep, rows.astype(f32) * scale, 0.0).astype(bf16)


def full_state(state):
    return jnp.concatenate(
        [state.astype(bf16), jnp.zeros((LANES - STATE_ROWS, VD), bf16)], axis=0
    )


def conv_kernel(heads, group, parts, *refs):
    place_ref = refs[0]
    pieces = refs[1 : 1 + parts]
    halo_ref, taps_ref, e1_ref, e2_ref, bias_ref = refs[1 + parts : 6 + parts]
    qk_ref, v_ref, mixed_ref, state_ref, total_ref = refs[6 + parts : 11 + parts]
    piece_scr, prev_scr, total_scr = refs[11 + parts :]
    chunk = pl.program_id(0)
    relative = chunk ^ place_ref[0]
    for j in range(parts):
        @pl.when(relative == j)
        def _(j=j):
            piece_scr[...] = pieces[j][...]

    first_lane, last_lane = group[0] * VD, (group[-1] + 1) * VD

    @pl.when(chunk == 0)
    def _():
        prev_scr[...] = halo_ref[:, first_lane:last_lane].astype(f32)
        total_scr[...] = jnp.zeros_like(total_scr)

    vw = heads * VD
    kw = heads * FK
    values = piece_scr[:, first_lane:last_lane]
    qk = piece_scr[:, vw : vw + 2 * kw]
    k = qk[:, kw:]
    qk_ref[...] = qk
    v_ref[...] = values
    wide = values.astype(f32)
    rows = wide.shape[0]
    at = lax.broadcasted_iota(jnp.int32, wide.shape, 0)
    before1 = prev_scr[7:8, :]
    before2 = prev_scr[6:7, :]
    lag1 = jnp.where(at == 0, before1, pltpu.roll(wide, 1, 0))
    lag2 = jnp.where(at == 0, before2, jnp.where(at == 1, before1, pltpu.roll(wide, 2, 0)))
    prev_scr[...] = wide[rows - 8 :, :]
    taps = taps_ref[:, first_lane:last_lane]
    mixed = (taps[0:1, :] * wide + taps[1:2, :] * lag1 + taps[2:3, :] * lag2).astype(bf16)
    mixed_ref[...] = mixed
    for i, h in enumerate(group):
        phi_t = features_t(k, e1_ref, e2_ref, bias_ref, h)
        state = mm(phi_t, mixed[:, i * VD : (i + 1) * VD])[:STATE_ROWS]
        state_ref[0, i] = state.astype(bf16)
        total_scr[i] += state

    @pl.when(chunk == pl.num_programs(0) - 1)
    def _():
        total_ref[...] = total_scr[...].astype(bf16)


def pre_kernel(heads, *refs):
    (
        _, qk_ref, mixed_ref, state_ref, e1_ref, e2_ref, bias_ref, e1t_ref, e2t_ref, biast_ref,
        local_ref, phi_ref, turned_ref, weight_ref, slope_ref, prefix_ref,
        run_scr,
    ) = refs

    @pl.when(pl.program_id(0) == 0)
    def _():
        run_scr[...] = jnp.zeros_like(run_scr)

    kw = heads * FK
    q = qk_ref[:, :kw]
    k = qk_ref[:, kw:]
    rows = q.shape[0]
    row = lax.broadcasted_iota(jnp.int32, (rows, rows), 0)
    col = lax.broadcasted_iota(jnp.int32, (rows, rows), 1)
    causal = row >= col
    for h in range(heads):
        lanes = slice(h * VD, (h + 1) * VD)
        first, second = features(q, e1_ref, e2_ref, bias_ref, h)
        phi = (first * second).astype(bf16)
        phi_ref[:, h * LANES : (h + 1) * LANES] = phi
        turned_ref[h] = features_t(q, e1t_ref, e2t_ref, biast_ref, h)
        u = mm_nt(q, head_only(k, h, FK ** -0.5))
        slope = 1.0 + u
        weight = jnp.where(causal, slope + 0.5 * u * u, 0.0).astype(bf16)
        weight_ref[h] = weight
        slope_ref[h] = jnp.where(causal, slope, 0.0).astype(bf16)
        prefix = run_scr[h].astype(bf16)
        prefix_ref[0, h] = prefix
        local = mm(weight, mixed_ref[:, lanes]) + mm(phi, full_state(prefix))
        local_ref[:, lanes] = local.astype(bf16)
        run_scr[h] += state_ref[0, h].astype(f32)


def mid_kernel(heads, parts, *refs):
    (
        place_ref, local_ref, phi_ref, turned_ref, carried_ref, ga_ref, gain_ref,
        qk_ref, weight_ref, e1k_ref, e2_ref, bias_ref,
        even_ref, odd_ref, ds_ref, gstate_ref, gtotal_ref, gain_sum_ref, halo_ref,
        gtotal_scr, attn_scr,
    ) = refs
    chunk = pl.program_id(0)
    relative = chunk ^ place_ref[0]

    @pl.when(chunk == 0)
    def _():
        gtotal_scr[...] = jnp.zeros_like(gtotal_scr)
        gain_sum_ref[...] = jnp.zeros_like(gain_sum_ref)

    for h in range(heads):
        lanes = slice(h * VD, (h + 1) * VD)
        phi = phi_ref[:, h * LANES : (h + 1) * LANES]
        summed = local_ref[:, lanes].astype(f32) + mm(phi, full_state(carried_ref[h]))
        scale = lax.rsqrt(jnp.mean(summed * summed, axis=-1, keepdims=True) + EPS)
        unit = summed * scale
        gain = gain_ref[0:1, lanes]
        attn_scr[:, lanes] = (unit * gain).astype(bf16)
        ga = ga_ref[0, :, lanes].astype(f32)
        gu = ga * unit
        gain_sum_ref[0:1, lanes] += jnp.sum(gu, axis=0, keepdims=True)
        ds = scale * (ga * gain - unit * jnp.mean(gu * gain, axis=-1, keepdims=True))
        ds = ds.astype(bf16)
        ds_ref[:, lanes] = ds
        gstate = mm(turned_ref[h], ds)[:STATE_ROWS]
        gstate_ref[0, h] = gstate.astype(bf16)
        gtotal_scr[h] += gstate

    @pl.when(chunk == 0)
    def _():
        kw = heads * FK
        vw = heads * VD
        qk = qk_ref[...]
        for h in range(heads):
            lanes = slice(h * VD, (h + 1) * VD)
            kfirst, ksecond = features(qk[:, kw:], e1k_ref, e2_ref, bias_ref, h)
            kphi = (kfirst * ksecond).astype(bf16)
            own = mm(kphi, full_state(gstate_ref[0, h]))
            top = mm_tn(weight_ref[h], ds_ref[:, lanes])
            halo_ref[:, lanes] = top[0:8] - own[0:8]
        halo_ref[:, vw:] = qk[0:8, :].astype(f32)

    @pl.when(relative % 2 == 0)
    def _():
        even_ref[relative // 2] = attn_scr[...]

    @pl.when(relative % 2 == 1)
    def _():
        odd_ref[relative // 2] = attn_scr[...]

    @pl.when(chunk == pl.num_programs(0) - 1)
    def _():
        gtotal_ref[...] = gtotal_scr[...].astype(bf16)


def post_kernel(heads, *refs):
    (
        _, qk_ref, mixed_ref, ds_ref, weight_ref, slope_ref, prefix_ref, carried_ref,
        e1q_ref, e2_ref, bias_ref,
        dqk_ref, dv_ref,
    ) = refs
    kw = heads * FK
    qk = qk_ref[...]
    q = qk[:, :kw]
    k = qk[:, kw:]
    dq = jnp.zeros(q.shape, f32)
    dk = jnp.zeros(q.shape, f32)
    for h in range(heads):
        lanes = slice(h * VD, (h + 1) * VD)
        ds = ds_ref[:, lanes]
        dw = mm_nt(ds, mixed_ref[:, lanes]).astype(bf16).astype(f32)
        du = (dw * slope_ref[h].astype(f32)).astype(bf16)
        dq += mm(du, head_only(k, h, FK ** -0.5))
        dk += mm_tn(du, head_only(q, h, FK ** -0.5))
        dv_ref[:, lanes] = mm_tn(weight_ref[h], ds).astype(bf16)
        state = full_state(prefix_ref[0, h].astype(f32) + carried_ref[h].astype(f32))
        first, second = features(q, e1q_ref, e2_ref, bias_ref, h)
        dq += features_pull(mm_nt(ds, state), first, second, e1q_ref, e2_ref, h)
    dqk_ref[:, :kw] = dq
    dqk_ref[:, kw:] = dk


def finish_kernel(heads, cut, parts, *refs):
    (
        place_ref, dqk_ref, qk_ref, v_ref, mixed_ref, dv_ref, gstate_ref, gin_ref,
        taps_ref, halo_ref, gain_ref, e1_ref, e2_ref, bias_ref,
        early_ref, late_ref, even_ref, odd_ref, sums_ref,
        run_scr, next_scr, mixed_scr, cols_scr,
    ) = refs
    step = pl.program_id(0)
    chunk = pl.num_programs(0) - 1 - step
    relative = chunk ^ place_ref[0]
    kw = heads * FK
    vw = heads * VD

    @pl.when(step == 0)
    def _():
        run_scr[...] = gin_ref[...].astype(f32)
        sums_ref[...] = jnp.zeros_like(sums_ref)
        sums_ref[3:4, :] = gain_ref[0:1, :]
        hk = jnp.concatenate([halo_ref[:, vw + kw :]] * 2, axis=0).astype(bf16)
        for h in range(heads):
            lanes = slice(h * VD, (h + 1) * VD)
            first, second = features(hk, e1_ref, e2_ref, bias_ref, h)
            phi = (first * second).astype(bf16)
            next_scr[:, lanes] = halo_ref[:, lanes] + mm(phi, full_state(gin_ref[h]))[0:8]

    k = qk_ref[:, kw:]
    dk = dqk_ref[:, kw:]
    for h in range(heads):
        lanes = slice(h * VD, (h + 1) * VD)
        first, second = features(k, e1_ref, e2_ref, bias_ref, h)
        phi = (first * second).astype(bf16)
        state = full_state(run_scr[h])
        mixed_scr[:, lanes] = dv_ref[:, lanes].astype(f32) + mm(phi, state)
        dphi = mm_nt(mixed_ref[:, lanes], state)
        dk += features_pull(dphi, first, second, e1_ref, e2_ref, h)
        run_scr[h] += gstate_ref[0, h].astype(f32)
    gm = mixed_scr[...]
    rows = gm.shape[0]
    at = lax.broadcasted_iota(jnp.int32, gm.shape, 0)
    after0 = next_scr[0:1, :]
    after1 = next_scr[1:2, :]
    lead1 = jnp.where(at == rows - 1, after0, pltpu.roll(gm, rows - 1, 0))
    lead2 = jnp.where(
        at == rows - 1, after1, jnp.where(at == rows - 2, after0, pltpu.roll(gm, rows - 2, 0))
    )
    next_scr[...] = gm[0:8, :]
    gv = taps_ref[0:1, :] * gm + taps_ref[1:2, :] * lead1 + taps_ref[2:3, :] * lead2
    values = v_ref[...].astype(f32)
    sums_ref[0:1, :] += jnp.sum(gm * values, axis=0, keepdims=True)
    sums_ref[1:2, :] += jnp.sum(lead1 * values, axis=0, keepdims=True)
    sums_ref[2:3, :] += jnp.sum(lead2 * values, axis=0, keepdims=True)
    cols_scr[:, :vw] = gv.astype(bf16)
    cols_scr[:, vw : vw + kw] = dqk_ref[:, :kw].astype(bf16)
    cols_scr[:, vw + kw :] = dk.astype(bf16)
    at_piece = relative // 2 + (relative % 2) * (parts // 2)
    early_ref[at_piece] = cols_scr[:, :cut]
    late_ref[at_piece] = cols_scr[:, cut:]

    @pl.when(relative % 2 == 0)
    def _():
        even_ref[relative // 2] = cols_scr[...]

    @pl.when(relative % 2 == 1)
    def _():
        odd_ref[relative // 2] = cols_scr[...]


def whole(shape):
    return pl.BlockSpec(shape, lambda *a, n=len(shape): (0,) * n)


def call(kernel, place, inputs, in_specs, out_shapes, out_specs, scratch, steps, flops, alias=None):
    return pl.pallas_call(
        kernel,
        out_shape=out_shapes,
        grid_spec=pltpu.PrefetchScalarGridSpec(
            num_scalar_prefetch=1,
            grid=(steps,),
            in_specs=in_specs,
            out_specs=out_specs,
            scratch_shapes=scratch,
        ),
        input_output_aliases=alias or {},
        compiler_params=pltpu.CompilerParams(
            dimension_semantics=("arbitrary",), vmem_limit_bytes=28 << 20
        ),
        cost_estimate=pl.CostEstimate(flops=0, bytes_accessed=0, transcendentals=0),
    )(place, *inputs)


def in_hbm(x):
    return pltpu.with_memory_space_constraint(x, pltpu.HBM)


def flip(x, axis, mask):
    n = lax.axis_size(axis)
    return lax.ppermute(x, axis, [(i, i ^ mask) for i in range(n)])


def held(x, *others):
    return lax.optimization_barrier((x,) + others)[0]


def scan_send(total, mask):
    return flip(total.astype(bf16), "seq", mask) if mask < lax.axis_size("seq") else None


def scan_take(before, total, got, mask, reverse):
    got = got.astype(f32)
    upper = (lax.axis_index("seq") & mask) != 0
    return before + jnp.where(upper != reverse, got, 0.0), total.astype(f32) + got


def arrange_kernel(parts, *refs):
    pieces = refs[1 : 1 + parts]
    kept_ref, sent_ref = refs[1 + parts :]
    rows = pieces[0].shape[0]
    step = pl.program_id(0)
    half = pl.num_programs(0) // 2
    for target, on in ((kept_ref, step < half), (sent_ref, step >= half)):
        @pl.when(on)
        def _(target=target):
            for j in range(parts):
                target[j * rows : (j + 1) * rows, :] = pieces[j][...]


def arranged(pieces, masks):
    n, place = lax.axis_size("seq"), lax.axis_index("seq")
    order = [0]
    for mask in masks[::-1]:
        order = order + [j | mask for j in order]
    order = jnp.asarray(np.array(order, np.int32)) ^ place.astype(jnp.int32)
    parts = len(pieces)
    rows, depth = pieces[0].shape
    length, width, half = parts * rows, depth // n, depth // 2
    if width % 128:
        full = jnp.concatenate(pieces, axis=0).reshape(length, n, width)
        full = jnp.take(full, order, axis=1).reshape(length, depth)
        return full[:, :half], full[:, half:]
    out = pltpu.HBM((length, half), bf16)
    mid = n // 2
    return call(
        functools.partial(arrange_kernel, parts),
        order,
        list(pieces),
        [pl.BlockSpec((rows, width), lambda i, o: (0, o[i]))] * parts,
        [out, out],
        [
            pl.BlockSpec((length, width), lambda i, o: (0, jnp.minimum(i, mid - 1))),
            pl.BlockSpec((length, width), lambda i, o: (0, jnp.maximum(i - mid, 0))),
        ],
        [], n, 0,
    )


class Halve:
    def __init__(self, turn, left, right, scale, extra=None):
        n = lax.axis_size("seq")
        self.masks = [1 << b for b in range(n.bit_length() - 1)]
        self.turn = turn and n > 2
        if self.turn:
            self.masks = self.masks[1:] + self.masks[:1]
        self.left, self.right, self.scale, self.extra = left, right, scale, extra

    def product(self, side, *others):
        left = held(self.left, *others) if others else self.left
        n = lax.axis_size("seq")
        width = 2 * self.right[0].shape[1] // n
        if self.turn:
            half = self.right[0].shape[1] // 2
            pair = [
                (mm_tn(left, right[:, side * half : (side + 1) * half]) * self.scale).astype(bf16)
                for right in self.right
            ]
            out = jnp.concatenate(
                [p[:, i * width : (i + 1) * width] for i in range(n // 4) for p in pair], axis=1
            )
        else:
            out = (mm_tn(left, self.right[side]) * self.scale).astype(bf16)
        if self.extra is not None:
            tail = (self.extra[:4] * self.scale).astype(bf16).reshape(4, -1, width)
            tail = tail.transpose(1, 0, 2).reshape(-1, width)
            out = jnp.concatenate([out, jnp.tile(tail, (1, n // 2))], axis=0)
        return out

    def begin(self, *others):
        self.first = self.product(1, *others)
        self.got = flip(self.first, "seq", self.masks[0])
        self.at = 1

    def keep(self, *others):
        self.kept = [self.product(0, *others)]
        return self.kept[0]

    def step(self, *others):
        got = held(self.got, *others)
        self.kept.append(got)
        if self.at == len(self.masks):
            self.out = sum(t.astype(f32) for t in self.kept)
            return self.out
        half = got.shape[1] // 2
        send = sum(t[:, half:].astype(f32) for t in self.kept).astype(bf16)
        self.got = flip(send, "seq", self.masks[self.at])
        self.at += 1
        self.kept = [t[:, :half] for t in self.kept]
        return send


def product_kernel(_, left_ref, right_ref, *refs):
    total = mm_nt(left_ref[...], right_ref[...])
    if len(refs) > 1:
        total += refs[0][...].astype(f32)
    refs[-1][...] = total.astype(bf16)


def product_nt(left, right, place, *more):
    height, width = left.shape[0], right.shape[0]
    tile = min(width, 1024)
    columns = pl.BlockSpec((height, tile), lambda i, p: (0, i))
    return call(
        product_kernel,
        place,
        [left, right, *more],
        [whole(left.shape), pl.BlockSpec((tile, right.shape[1]), lambda i, p: (i, 0))]
        + [columns] * len(more),
        [jax.ShapeDtypeStruct((height, width), bf16)],
        [columns],
        [], width // tile, 0,
    )[0]


def masks_of(first):
    n = lax.axis_size("seq")
    masks = [1 << b for b in range(n.bit_length() - 1)]
    return masks[first:] + masks[:first]


def per_device(tokens_in, w_query, w_key, w_value, w_output, conv_taps, norm_gain, grad_out):
    nt, ns = lax.axis_size("tensor"), lax.axis_size("seq")
    rows, depth = tokens_in.shape
    length = rows * nt
    kw, vw = w_query.shape[1], w_value.shape[1]
    heads = vw // VD
    grad_scale = float(length * ns) ** -0.5
    place = lax.axis_index("tensor").reshape(1).astype(jnp.int32)
    e1q, e1k, e2, bias = feature_tables(heads)
    turned_q, turned_k, turned2 = e1q.T, e1k.T, e2.T
    turned_bias = jnp.pad(bias[:2].T, ((0, 0), (0, 126)))
    (
        e1q, e1k, e2, bias, turned_q, turned_k, turned2, turned_bias, conv_taps, norm_gain
    ) = (
        pltpu.with_memory_space_constraint(x, pltpu.HBM)
        for x in (
            e1q, e1k, e2, bias, turned_q, turned_k, turned2, turned_bias, conv_taps,
            norm_gain.reshape(1, -1),
        )
    )
    evens, odds = list(range(0, nt, 2)), list(range(1, nt, 2))

    far = {j: flip(tokens_in, "tensor", j) for j in evens[1:]}
    near = flip(tokens_in, "tensor", 1)
    near_cot = flip(grad_out, "tensor", 1)
    tail = held(tokens_in, near)[rows - 2 :]
    above = sum(
        lax.ppermute(
            tail, ("seq", "tensor"), [(s * nt + nt - 1, (s + 1) * nt + i) for s in range(ns - 1)]
        )
        for i in range(nt)
    )
    cw = vw + 2 * kw
    joined = [held(w, near) for w in (w_value, w_query, w_key)]
    weights = lax.optimization_barrier(jnp.concatenate(joined, axis=1))
    project = lambda piece: mm(piece, weights).astype(bf16)
    pull = lambda piece: mm_nt(piece, w_output).astype(bf16)
    halo = jnp.pad(mm(above, w_value).astype(bf16), ((6, 0), (0, 0)))
    tokens, cotangent = [tokens_in, near], [grad_out, near_cot]
    projected = [project(tokens_in), project(near)]
    pulled = [pull(grad_out), pull(near_cot)]
    for j in evens[1:]:
        piece = held(far[j], halo, *projected, *pulled)
        tokens += [piece, flip(piece, "tensor", 1)]
    projected += [project(piece) for piece in tokens[2:]]
    cot_from = held(grad_out, projected[2])
    far_cot = {j: flip(cot_from, "tensor", j) for j in evens[1:]}

    state_shape = (heads, STATE_ROWS, VD)
    at_chunk = lambda i, p: (i, 0)
    at_state = lambda i, p: (i, 0, 0, 0)
    on_chunk = lambda width: pl.BlockSpec((rows, width), at_chunk)
    state_spec = pl.BlockSpec((1,) + state_shape, at_state)
    square_spec = pl.BlockSpec((heads, rows, rows), lambda i, p: (0, i, 0))
    tables = [whole(e1q.shape), whole(e2.shape), whole(bias.shape)]
    turned_tables = [whole(turned_q.shape), whole(turned2.shape), whole(turned_bias.shape)]
    turned_spec = pl.BlockSpec((heads, LANES, rows), lambda i, p: (0, 0, i))
    shape = jax.ShapeDtypeStruct
    states_shape = shape((nt,) + state_shape, bf16)
    qk, values, mixed, states, total = call(
        functools.partial(conv_kernel, heads, list(range(heads)), nt),
        place,
        projected + [halo, conv_taps, turned_k, turned2, turned_bias],
        [whole((rows, cw))] * nt + [whole((8, vw)), whole((3, vw))] + turned_tables,
        [
            shape((length, 2 * kw), bf16),
            shape((length, vw), bf16),
            shape((length, vw), bf16),
            states_shape,
            shape(state_shape, bf16),
        ],
        [on_chunk(2 * kw), on_chunk(vw), on_chunk(vw), state_spec, whole(state_shape)],
        [pltpu.VMEM((rows, cw), bf16), pltpu.VMEM((8, vw), f32), pltpu.VMEM(state_shape, f32)],
        nt, 2 * length * vw * 256 * 3,
    )

    before = jnp.zeros(state_shape, f32)
    mask = 1
    got = scan_send(total, mask)
    pinned = lambda dims, kind: pltpu.HBM(dims, kind)
    local, phi, phi_t, weight, slope, prefix = call(
        functools.partial(pre_kernel, heads),
        place,
        [qk, mixed, states, e1q, e2, bias, turned_q, turned2, turned_bias],
        [on_chunk(2 * kw), on_chunk(vw), state_spec] + tables + turned_tables,
        [
            pinned((length, vw), bf16),
            pinned((length, heads * LANES), bf16),
            pinned((heads, LANES, length), bf16),
            pinned((heads, length, rows), bf16),
            pinned((heads, length, rows), bf16),
            states_shape,
        ],
        [
            on_chunk(vw), on_chunk(heads * LANES), turned_spec, square_spec, square_spec,
            state_spec,
        ],
        [pltpu.VMEM(state_shape, f32)],
        nt, 2 * length * vw * 256 * 5,
    )
    got = held(got, local)
    ordered = lambda pieces: [pieces[j] for j in evens + odds]
    while got is not None:
        before, total = scan_take(before, total, got, mask, False)
        mask *= 2
        got = scan_send(total, mask)
        if mask * 2 == ns:
            for j in evens[1:]:
                piece = held(far_cot[j], total)
                cotangent += [piece, flip(piece, "tensor", 1)]
            pulled += [pull(piece) for piece in cotangent[2:]]
            by_place = [pulled[j] for j in evens + odds]
            grad_attn = jnp.stack(by_place)
            ready = ordered(cotangent)
            ready[0] = held(ready[0], grad_attn)
            cot_for = arranged(ready, masks_of(0))
            got = held(got, *cot_for)
    carried = before.astype(bf16)

    half_shape = shape((nt // 2, rows, vw), bf16)
    slot = lambda j: (j >> 1) + (j & 1) * (nt // 2)
    attn_even, attn_odd, ds, gstates, gtotal, gain_sum, halo_out = call(
        functools.partial(mid_kernel, heads, nt),
        place,
        [
            local, phi, phi_t, carried, grad_attn, norm_gain, qk, weight, e1k, e2,
            bias,
        ],
        [
            on_chunk(vw),
            on_chunk(heads * LANES),
            turned_spec,
            whole(state_shape),
            pl.BlockSpec((1, rows, vw), lambda i, p: (slot(i ^ p[0]), 0, 0)),
            whole((1, vw)),
            whole((16, 2 * kw)),
            whole((heads, rows, 128)),
        ]
        + tables,
        [
            half_shape, half_shape, shape((length, vw), bf16), states_shape,
            shape(state_shape, bf16), shape((8, vw), f32), shape((8, vw + 2 * kw), f32),
        ],
        [
            whole(half_shape.shape), whole(half_shape.shape), on_chunk(vw), state_spec,
            whole(state_shape), whole((8, vw)), whole((8, vw + 2 * kw)),
        ],
        [pltpu.VMEM(state_shape, f32), pltpu.VMEM((rows, vw), bf16)],
        nt, 2 * length * vw * 256 * 2,
    )

    attn_all = jnp.concatenate([attn_even.reshape(-1, vw), attn_odd.reshape(-1, vw)], axis=0)
    ready = ordered(tokens)
    ready[0] = held(ready[0], gtotal)
    tokens_for = arranged(ready, masks_of(0))
    out_halve = Halve(False, attn_all, cot_for, grad_scale)
    after = jnp.zeros(state_shape, f32)
    got = scan_send(gtotal, 1)
    halo_in = lax.ppermute(halo_out, "seq", [(i + 1, i) for i in range(ns - 1)])
    out_odd = mm(attn_odd.reshape(-1, vw), w_output).astype(bf16)
    out_got = flip(out_odd, "tensor", 1)
    mask = 1
    while got is not None:
        cover = [out_odd, *tokens_for] if mask == 1 else [kept] if mask == 2 else [dv]
        after, gtotal = scan_take(after, gtotal, held(got, *cover), mask, True)
        mask *= 2
        got = scan_send(gtotal, mask)
        if mask == 2:
            out_flips = []
            out_rows = mm(attn_even.reshape(-1, vw), w_output) + held(out_got, gtotal).astype(f32)
            out_rows = out_rows.astype(bf16)
            for i in range(1, nt // 2):
                out_flips.append(flip(out_rows[i * rows : (i + 1) * rows], "tensor", 2 * i))
            out_halve.begin(out_rows)
            kept = out_halve.keep(out_halve.first)
        if mask == 4 or (mask == 2 and ns == 2):
            dqk, dv = call(
                functools.partial(post_kernel, heads),
                place,
                [
                    held(qk, gtotal), in_hbm(mixed), ds, in_hbm(weight), in_hbm(slope),
                    in_hbm(prefix), carried, e1q, e2, bias,
                ],
                [
                    on_chunk(2 * kw), on_chunk(vw), on_chunk(vw), square_spec, square_spec,
                    state_spec, whole(state_shape),
                ]
                + tables,
                [shape((length, 2 * kw), f32), shape((length, vw), bf16)],
                [on_chunk(2 * kw), on_chunk(vw)],
                [],
                nt, 2 * length * vw * 256 * 8,
            )
    gin = after.astype(bf16)
    dqk = held(dqk, out_halve.step(gin))

    last = lambda i, p: (nt - 1 - i, 0)
    from_last = lambda width: pl.BlockSpec((rows, width), last)
    cut = cw * 6 // 10 // 128 * 128
    early, late, cols_even, cols_odd, sums = call(
        functools.partial(finish_kernel, heads, cut, nt),
        place,
        [dqk, qk, values, mixed, dv, gstates, gin, conv_taps, halo_in, gain_sum, e1k, e2, bias],
        [
            from_last(2 * kw), from_last(2 * kw), from_last(vw), from_last(vw), from_last(vw),
            pl.BlockSpec((1,) + state_shape, lambda i, p: (nt - 1 - i, 0, 0, 0)),
            whole(state_shape), whole((3, vw)), whole((8, vw + 2 * kw)), whole((8, vw)),
        ]
        + tables,
        [
            shape((nt, rows, cut), bf16), shape((nt, rows, cw - cut), bf16),
            shape((nt // 2, rows, cw), bf16), shape((nt // 2, rows, cw), bf16),
            shape((8, vw), f32),
        ],
        [
            whole((nt, rows, cut)), whole((nt, rows, cw - cut)),
            whole((nt // 2, rows, cw)), whole((nt // 2, rows, cw)), whole((8, vw)),
        ],
        [
            pltpu.VMEM(state_shape, f32), pltpu.VMEM((8, vw), f32),
            pltpu.VMEM((rows, vw), f32), pltpu.VMEM((rows, cw), bf16),
        ],
        nt, 2 * length * vw * 256 * 6,
    )
    first = Halve(False, early.reshape(length, cut), tokens_for, grad_scale)
    out_flips = [held(got, early) for got in out_flips]
    steps = len(out_halve.masks)
    first = Halve(False, early.reshape(length, cut), tokens_for, grad_scale)
    first.begin(*out_flips)
    second = Halve(True, late.reshape(length, cw - cut), tokens_for, grad_scale, sums)
    done = out_halve.step(first.first) if steps > 2 else first.first
    second.begin(done)
    in_odd = product_nt(held(cols_odd, second.first).reshape(-1, cw), weights, place)
    in_got = held(flip(in_odd, "tensor", 1), in_odd)
    in_rows = mm_nt(cols_even.reshape(-1, cw), weights) + in_got.astype(f32)
    in_rows = in_rows.astype(bf16)
    in_flips = []
    for i in range(1, nt // 2):
        in_flips.append(flip(in_rows[i * rows : (i + 1) * rows], "tensor", 2 * i))
    done = first.keep(in_rows)
    done = first.step(done)
    done = second.keep(done)
    done = second.step(done)
    layer_out = held(out_rows, done)[:rows].astype(f32)
    for got in out_flips:
        layer_out += got.astype(f32)
    done = layer_out = layer_out.astype(bf16)
    for k in range(1, steps):
        done = first.step(done) if k < steps - 1 else done
        done = second.step(done)
        if k < steps - 1 or steps == 2:
            done = out_halve.step(done)
        if k == steps - 2 or steps == 2:
            grad_in = in_rows[:rows].astype(f32)
            for got in in_flips:
                grad_in += held(got, done).astype(f32)
            done = grad_in = grad_in.astype(bf16)
    first.step(done)
    while not hasattr(out_halve, "out"):
        out_halve.step(done)
    grad_wo = out_halve.out.astype(bf16)
    low, high = first.out.astype(bf16), second.out[: cw - cut].astype(bf16)
    sums = second.out[cw - cut :]
    sums = jnp.concatenate(jnp.split(sums, sums.shape[0] // 4, axis=0), axis=1)
    more = vw - cut
    grad_wv = jnp.concatenate([low.T, high[:more].T], axis=1)
    grad_wq = high[more : more + kw].T
    grad_wk = high[more + kw :].T
    return (layer_out, grad_in, grad_wq, grad_wk, grad_wv, grad_wo, sums[0:3], sums[3])


def solution(mesh):
    return jax.shard_map(
        per_device,
        mesh=mesh,
        in_specs=(
            P(("seq", "tensor"), None),
            P(None, "tensor"),
            P(None, "tensor"),
            P(None, "tensor"),
            P("tensor", None),
            P(None, "tensor"),
            P("tensor"),
            P(("seq", "tensor"), None),
        ),
        out_specs=(
            P(("seq", "tensor"), None),
            P(("seq", "tensor"), None),
            P("seq", "tensor"),
            P("seq", "tensor"),
            P("seq", "tensor"),
            P("tensor", "seq"),
            P(None, "tensor"),
            P("tensor"),
        ),
        check_vma=False,
    )
```
